128 devices in a mesh: ulysses: 8 (over z, core), dp: 16 (over x, y).
Axes of the slice: x: 4, y: 4, z: 4, core: 2. Of those that a mesh axis runs over, the one named last changes fastest.
Arguments:
- tokens: bfloat16 [16, 2048, 2048], P('dp', 'ulysses'), may hold values from -60 to 60
- d_out: bfloat16 [16, 2048, 2048], P('dp', 'ulysses'), may hold values from -6 to 6
- lengths: int32 [16, 21], P('dp'), may hold values from 1 to 384, 2048 in all within a row
- gain: bfloat16 [2048], P('dp'), may hold values from 0.5 to 1.5
- w_qkv: bfloat16 [2048, 1536], P('dp'), may hold values from -16 to 16
- w_out: bfloat16 [2048, 1024], P('dp'), may hold values from -0.1875 to 0.1875
Outputs:
- d_tokens: bfloat16 [16, 2048, 2048], P('dp', 'ulysses')
- d_w_qkv: float32 [2048, 1536], P(('ulysses', 'dp'))
- d_w_out: float32 [2048, 1024], P(('ulysses', 'dp'))
- d_gain: float32 [2048], P(('ulysses', 'dp'))
The draws below stay inside these ranges and needn't reach their ends.
Inputs may be any that keep to these rules, and one draw needn't show every extreme that they name: Each row holds whole document lengths of 1 to 384 tokens that sum to 2048; the longest is exactly 384.
All inputs are finite; a program needn't handle non-finite values.
Results may differ from the reference program's by a relative error of at most 0.01.
The reference program's roundings to bfloat16 on the way count: a program that leaves them out, or rounds other values in their place, can miss the bound.
Values may be sent and summed in bfloat16 or wider, within the bound.
A program may use at most 128 MiB of HBM per device.

```python
import math
import jax
import jax.numpy as jnp
import numpy as np
from jax import lax

D = 2048
HEADS = 16
KV_HEADS = 4
HEAD_DIM = 64
DOC_MOST = 384
SEQ = 2048
GROUPS = 16
DOCS = 21
ALL_TOKENS = 32768
QW = 1024
KW = 256
QKVW = 1536
N_ULYSSES = 8


def draw_tokens(key, part):
    key_base, key_rows, key_cols = jax.random.split(key, 3)
    base = jax.random.normal(key_base, (GROUPS, SEQ, D), jnp.float32)
    row_scale = jnp.exp(jax.random.uniform(key_rows, (GROUPS, SEQ, 1), jnp.float32, 0.0, math.log(10.0)))
    col_scale = jnp.exp(jax.random.uniform(key_cols, (1, 1, D), jnp.float32, 0.0, math.log(10.0))) / 3.0
    return jnp.clip(base * row_scale * col_scale, -60.0, 60.0).astype(jnp.bfloat16)


def draw_w_qkv(key, part):
    key_base = jax.random.fold_in(key, 0)
    base = jnp.clip(jax.random.normal(key_base, (D, QKVW), jnp.float32), -6.0, 6.0) * D ** (-0.5)
    return jnp.clip(base, -16.0, 16.0).astype(jnp.bfloat16)


def levels(stream_key, dims, shards, least, high):
    def one(axis_at, shards_of):
        steps = jax.random.uniform(jax.random.fold_in(jax.random.fold_in(stream_key, 6), axis_at), (shards_of,), jnp.float32, least / len(shards), high / len(shards))
        return jnp.repeat(jnp.exp(steps), dims[axis_at] // shards_of).reshape((-1,) + (1,) * (len(dims) - axis_at - 1))

    loudness = one(*shards[0])
    for cut in shards[1:]:
        loudness = loudness * one(*cut)
    return loudness


def profile(amount, total, limit, slope):
    loads = [(1 << 20) // math.isqrt(standing ** slope) + 1 for standing in range(2, amount + 1)]
    surplus, holding = total - limit - (amount - 1), [1] * (amount - 1)
    while surplus > 0:
        free = [i for i in range(amount - 1) if holding[i] < limit]
        whole, left = sum([loads[i] for i in free]), surplus
        for i in free:
            addition = min(limit - holding[i], max(1, left * loads[i] // whole), surplus)
            holding[i] = holding[i] + addition
            surplus = surplus - addition
    return np.array([limit] + holding)


def uneven_parts(rng, number_of, total, most, slope):
    if number_of == 2:
        one = jax.random.randint(rng, (), max(1, total - most), min(most, total - 1) + 1)
        return jnp.stack([one, total - one])
    sizes = jnp.asarray(profile(number_of, total, most, slope), jnp.int32)
    pairs = (number_of - 1) // 2
    giver, receiver = sizes[1:1 + 2 * pairs:2], sizes[2:2 + 2 * pairs:2]
    margin = jnp.minimum(giver - 1, most - receiver)
    moved = jax.random.randint(jax.random.fold_in(rng, 1), (pairs,), 0, 1 << 20) % (margin + 1)
    sizes = sizes.at[1:1 + 2 * pairs:2].set(giver - moved).at[2:2 + 2 * pairs:2].set(receiver + moved)
    return sizes[jax.random.permutation(jax.random.fold_in(rng, 2), number_of)]


def noise(stream_key, shape, scale, most, shards=(), held_as=jnp.bfloat16):
    level = levels(stream_key, shape, shards, -0.22, 0.18) if shards else 1.0
    array = jax.random.normal(stream_key, shape, jnp.float32) * scale * level
    return jnp.minimum(jnp.maximum(array, -most), most).astype(held_as)


def setup_inputs(seed: int = 0) -> dict:
    key_list = jax.random.split(jax.random.key(seed), 7)
    return {
        "tokens": draw_tokens(jax.random.fold_in(key_list[6], 71), 0),
        "d_out": noise(key_list[1], (GROUPS, SEQ, D), 1.0, 6.0, ((0, 16), (1, 8))),
        "lengths": jax.vmap(lambda own: uneven_parts(own, DOCS, SEQ, DOC_MOST, 2))(jax.random.split(key_list[2], GROUPS)).reshape((GROUPS, DOCS)).astype(jnp.int32),
        "gain": jnp.clip(1.0 + 0.1 * jax.random.normal(key_list[3], (D,), jnp.float32), 0.5, 1.5).astype(jnp.bfloat16),
        "w_qkv": draw_w_qkv(jax.random.fold_in(key_list[6], 71), 0),
        "w_out": noise(key_list[5], (D, QW), QW ** -0.5, 0.1875, ((0, 16),)),
    }


EPS = 1e-05
ROPE_BASE = 500000.0

def doc_positions(doc_lengths, length):
    bounds = (jnp.cumsum(doc_lengths) - doc_lengths).astype(jnp.int32)
    places = jnp.arange(length, dtype=jnp.int32)
    begins = lax.optimization_barrier(jnp.max(jnp.where(bounds[None, :] <= places[:, None], bounds[None, :], 0), axis=1)).astype(jnp.int32)
    return (begins, (places - begins).astype(jnp.int32))

def rotary_tables(places):
    inverse = ROPE_BASE ** (-jnp.arange(0, HEAD_DIM, 2).astype(jnp.float32) / HEAD_DIM)
    angles = places.astype(jnp.float32)[:, None] * inverse[None, :]
    angles = jnp.concatenate([angles, angles], axis=1)
    return (jnp.cos(angles), jnp.sin(angles))

def rotate(values, cos_table, sin_table):
    half_dim = HEAD_DIM // 2
    turned = jnp.concatenate([-values[..., half_dim:], values[..., :half_dim]], axis=-1)
    return values * cos_table[:, None, :] + turned * sin_table[:, None, :]

def attend(query_head, key_head, value_head, grad_head, begins):
    length, heads_here, _ = query_head.shape
    block_len = min(512, length)
    blocks = length // block_len
    scale = HEAD_DIM ** (-0.5)
    filler = jnp.zeros((block_len, HEAD_DIM), key_head.dtype)
    key_blocks = jnp.concatenate([filler, key_head], axis=0).reshape(blocks + 1, block_len, HEAD_DIM)
    key_window = jnp.concatenate([key_blocks[:-1], key_blocks[1:]], axis=1)
    value_blocks = jnp.concatenate([filler, value_head], axis=0).reshape(blocks + 1, block_len, HEAD_DIM)
    value_window = jnp.concatenate([value_blocks[:-1], value_blocks[1:]], axis=1)
    query_blocks = query_head.reshape(blocks, block_len * heads_here, HEAD_DIM)
    grad_blocks = grad_head.reshape(blocks, block_len * heads_here, HEAD_DIM)
    begin_blocks = begins.reshape(blocks, block_len)

    def one_block(inputs):
        block_index, query_b, grad_b, key_w, value_w, begin_b = inputs
        query_pos = block_index * block_len + jnp.arange(block_len, dtype=jnp.int32)
        key_pos = (block_index - 1) * block_len + jnp.arange(2 * block_len, dtype=jnp.int32)
        allowed = (key_pos[None, :] >= begin_b[:, None]) & (key_pos[None, :] <= query_pos[:, None])
        allowed = jnp.broadcast_to(allowed[:, None, :], (block_len, heads_here, 2 * block_len))
        allowed = allowed.reshape(block_len * heads_here, 2 * block_len)
        scores = jnp.einsum('qd,kd->qk', query_b.astype(jnp.float32), key_w.astype(jnp.float32)) * scale
        scores = jnp.where(allowed, scores, -1e+30)
        peak = lax.optimization_barrier(jnp.max(scores, axis=1, keepdims=True))
        weights = jnp.where(allowed, jnp.exp(scores - peak), 0.0)
        shares = weights / lax.optimization_barrier(jnp.sum(weights, axis=1, keepdims=True))
        shares_low = shares.astype(jnp.bfloat16)
        mixed = jnp.dot(shares_low, value_w, preferred_element_type=jnp.float32)
        row_dot = lax.optimization_barrier(jnp.sum(grad_b.astype(jnp.float32) * mixed, axis=1, keepdims=True))
        d_shares = jnp.einsum('qd,kd->qk', grad_b.astype(jnp.float32), value_w.astype(jnp.float32))
        d_scores = (shares * (d_shares - row_dot) * scale).astype(jnp.bfloat16)
        d_query = jnp.dot(d_scores, key_w, preferred_element_type=jnp.float32)
        d_keys = jnp.einsum('qk,qd->kd', d_scores.astype(jnp.float32), query_b.astype(jnp.float32))
        d_values = jnp.einsum('qk,qd->kd', shares_low.astype(jnp.float32), grad_b.astype(jnp.float32))
        return (mixed.astype(jnp.bfloat16), d_query, d_keys, d_values)
    block_ids = jnp.arange(blocks, dtype=jnp.int32)
    mixed, d_query, d_keys, d_values = lax.map(one_block, (block_ids, query_blocks, grad_blocks, key_window, value_window, begin_blocks))
    mixed = mixed.reshape(length, heads_here * HEAD_DIM)
    d_query = d_query.reshape(length, heads_here, HEAD_DIM)
    pad_front = ((1, 0), (0, 0), (0, 0))
    pad_back = ((0, 1), (0, 0), (0, 0))
    d_keys = (jnp.pad(d_keys[:, :block_len], pad_back) + jnp.pad(d_keys[:, block_len:], pad_front))[1:]
    d_values = (jnp.pad(d_values[:, :block_len], pad_back) + jnp.pad(d_values[:, block_len:], pad_front))[1:]
    return (mixed, d_query, d_keys.reshape(length, HEAD_DIM), d_values.reshape(length, HEAD_DIM))

def head_side(head_block, begins, places, heads_here):
    length = head_block.shape[0]
    q_width = heads_here * HEAD_DIM
    query_head = head_block[:, :q_width].reshape(length, heads_here, HEAD_DIM)
    key_head = head_block[:, q_width:q_width + HEAD_DIM]
    value_head = head_block[:, q_width + HEAD_DIM:q_width + 2 * HEAD_DIM]
    grad_head = head_block[:, q_width + 2 * HEAD_DIM:].reshape(length, heads_here, HEAD_DIM)
    mixed, d_query, d_keys, d_values = attend(query_head, key_head, value_head, grad_head, begins)
    cos_table, sin_table = rotary_tables(places)
    d_query = rotate(d_query, cos_table, -sin_table).astype(jnp.bfloat16).reshape(length, q_width)
    d_keys = rotate(d_keys[:, None, :], cos_table, -sin_table)[:, 0, :].astype(jnp.bfloat16)
    d_values = d_values.astype(jnp.bfloat16)
    return jnp.concatenate([mixed, d_query, d_keys, d_values], axis=1)

def reference(tokens, d_out, lengths, gain, w_qkv, w_out):
    groups = N_ULYSSES
    heads_here = HEADS // groups
    repeat = groups // KV_HEADS
    q_width = heads_here * HEAD_DIM
    factor = 1.0 / math.sqrt(ALL_TOKENS)
    gain_wide = gain.astype(jnp.float32)

    def per_group(carry, inputs):
        token_rows, grad_rows, doc_lengths = inputs
        rows = token_rows.shape[0]
        begins, places = doc_positions(doc_lengths, rows)
        wide_rows = token_rows.astype(jnp.float32)
        inv_rms = lax.rsqrt(lax.optimization_barrier(jnp.mean(wide_rows * wide_rows, axis=1, keepdims=True)) + EPS)
        unit_rows = wide_rows * inv_rms
        normed = (unit_rows * gain_wide[None, :]).astype(jnp.bfloat16)
        projected = jnp.dot(normed, w_qkv, preferred_element_type=jnp.float32)
        cos_table, sin_table = rotary_tables(places)
        query = rotate(projected[:, :QW].reshape(rows, HEADS, HEAD_DIM), cos_table, sin_table).astype(jnp.bfloat16)
        key_rows = rotate(projected[:, QW:QW + KW].reshape(rows, KV_HEADS, HEAD_DIM), cos_table, sin_table).astype(jnp.bfloat16)
        value_rows = projected[:, QW + KW:].astype(jnp.bfloat16).reshape(rows, KV_HEADS, HEAD_DIM)
        key_rows = jnp.repeat(key_rows, repeat, axis=1)
        value_rows = jnp.repeat(value_rows, repeat, axis=1)
        d_attn = jnp.dot(grad_rows, w_out, preferred_element_type=jnp.float32).astype(jnp.bfloat16)
        packed = jnp.concatenate([query.reshape(rows, groups, q_width), key_rows, value_rows, d_attn.reshape(rows, groups, q_width)], axis=2)
        slots = jnp.transpose(packed, (1, 0, 2))
        outgoing = lax.map(lambda block: head_side(block, begins, places, heads_here), slots)
        returned = jnp.transpose(outgoing, (1, 0, 2))
        mixed_rows = returned[:, :, :q_width].reshape(rows, QW)
        dq_rows = returned[:, :, q_width:2 * q_width].reshape(rows, QW)
        dk_rows = returned[:, :, 2 * q_width:2 * q_width + HEAD_DIM].astype(jnp.float32)
        dk_rows = dk_rows.reshape(rows, KV_HEADS, repeat, HEAD_DIM).sum(axis=2).astype(jnp.bfloat16).reshape(rows, KW)
        dv_rows = returned[:, :, 2 * q_width + HEAD_DIM:].astype(jnp.float32)
        dv_rows = dv_rows.reshape(rows, KV_HEADS, repeat, HEAD_DIM).sum(axis=2).astype(jnp.bfloat16).reshape(rows, KW)
        d_proj = jnp.concatenate([dq_rows, dk_rows, dv_rows], axis=1)
        grad_qkv = jnp.einsum('td,tc->dc', normed.astype(jnp.float32), d_proj.astype(jnp.float32))
        grad_out = jnp.einsum('td,tc->dc', grad_rows.astype(jnp.float32), mixed_rows.astype(jnp.float32))
        d_normed = jnp.einsum('tc,dc->td', d_proj.astype(jnp.float32), w_qkv.astype(jnp.float32))
        grad_gain = lax.optimization_barrier(jnp.sum(d_normed * unit_rows, axis=0))
        scaled = d_normed * gain_wide[None, :]
        d_rows = inv_rms * (scaled - unit_rows * lax.optimization_barrier(jnp.mean(scaled * unit_rows, axis=1, keepdims=True)))
        d_tokens = (grad_rows.astype(jnp.float32) + d_rows).astype(jnp.bfloat16)
        return ((carry[0] + grad_qkv, carry[1] + grad_out, carry[2] + grad_gain), d_tokens)
    start = (jnp.zeros((D, QKVW), jnp.float32), jnp.zeros((D, QW), jnp.float32), jnp.zeros((D,), jnp.float32))
    summed, d_tokens = lax.scan(per_group, start, (tokens, d_out, lengths))
    return (d_tokens, summed[0] * factor, summed[1] * factor, summed[2] * factor)
```

```python
import functools
import math

import jax
import jax.numpy as jnp
from jax import lax
from jax.experimental import pallas as pl
from jax.experimental.pallas import tpu as pltpu
from jax.sharding import PartitionSpec as P

HEADS = 16
KV_HEADS = 4
HEAD_DIM = 64
D = 2048
SEQ = 2048
ROWS = 256
QW = 1024
KW = 256
NU = 8
ND = 16
EPS = 1e-05
ROPE_BASE = 500000.0
MESH = pl.DeviceIdType.MESH
F32 = jnp.float32
BF16 = jnp.bfloat16


def doc_positions(doc_lengths, length):
    bounds = jnp.cumsum(doc_lengths) - doc_lengths
    places = jnp.arange(length, dtype=jnp.int32)
    begins = jnp.max(jnp.where(bounds[None, :] <= places[:, None], bounds[None, :], 0), axis=1)
    return begins, places - begins


def rotary_tables_t(places):
    inverse = ROPE_BASE ** (-jnp.arange(0, HEAD_DIM, 2).astype(F32) / HEAD_DIM)
    angles = inverse[:, None] * places.astype(F32)[None, :]
    cos, sin = jnp.cos(angles), jnp.sin(angles)
    return jnp.concatenate([cos, cos], axis=0), jnp.concatenate([sin, sin], axis=0)


def remote(src, dst, send_sem, recv_sem, u, d):
    return pltpu.make_async_remote_copy(
        src_ref=src, dst_ref=dst, send_sem=send_sem, recv_sem=recv_sem,
        device_id={"ulysses": u, "dp": d}, device_id_type=MESH,
    )


def gather_kernel(tok, dout, wqkv, wout, gain, T, G, W, WO, GN,
                  zs, zr, ps, pr, ws, wr, os_, or_, gs, gr, wps, wpr, loc):
    u = lax.axis_index("ulysses")
    d = lax.axis_index("dp")
    z, c = u // 2, u % 2
    right = ((z + 1) % 4) * 2 + c
    left = ((z + 3) % 4) * 2 + c
    far = ((z + 2) % 4) * 2 + c
    mate = z * 2 + (1 - c)

    barrier = pltpu.get_barrier_semaphore()
    for peer in (right, left, mate):
        pl.semaphore_signal(barrier, inc=1, device_id={"ulysses": peer, "dp": d}, device_id_type=MESH)

    @pl.loop(1, ND)
    def _(k):
        pl.semaphore_signal(barrier, inc=1, device_id={"ulysses": u, "dp": (d + k) % ND}, device_id_type=MESH)

    pl.semaphore_wait(barrier, 3 + ND - 1)

    H = ROWS // 2
    A, B = pl.ds(0, H), pl.ds(H, H)
    srcs, dsts = (tok, dout), (T, G)

    def own(a, slot, rows, to):
        return remote(srcs[a].at[rows], dsts[a].at[u, rows], zs.at[a, slot], zr.at[a, slot], to, d)

    def fwd(a, slot, frm, rows, to):
        return remote(dsts[a].at[frm, rows], dsts[a].at[frm, rows], zs.at[a, slot], zr.at[a, slot], to, d)

    def relay(a, slot, frm, rows):
        return remote(dsts[a].at[frm, rows], dsts[a].at[frm, rows], ps.at[a, slot], pr.at[a, slot], mate, d)

    def own_relay(a):
        return remote(srcs[a], dsts[a].at[u], ps.at[a, 6], pr.at[a, 6], mate, d)

    def start_own(a):
        own(a, 0, A, right).start()
        own(a, 3, B, left).start()
        own(a, 1, B, right).start()
        own(a, 2, A, left).start()
        own_relay(a).start()

    start_own(0)

    HW = wqkv.shape[0] // 2

    def w_copy(k):
        to = (d + k) % ND
        return remote(wqkv.at[pl.ds(c * HW, HW)], W.at[d, c], ws.at[k], wr.at[k], u, to)

    def o_copy(k):
        to = (d + k) % ND
        return remote(wout.at[:, pl.ds(pl.multiple_of(u * 128, 128), 128)], WO.at[d], os_.at[k], or_.at[k], u, to)

    def g_copy(k):
        to = (d + k) % ND
        return remote(gain, GN.at[d], gs.at[k], gr.at[k], u, to)

    @pl.loop(1, ND)
    def _(k):
        g_copy(k).start()
        o_copy(k).start()
        w_copy(k).start()

    locals_ = [
        pltpu.make_async_copy(tok, T.at[u], loc.at[0]),
        pltpu.make_async_copy(dout, G.at[u], loc.at[1]),
        pltpu.make_async_copy(wqkv.at[pl.ds(c * HW, HW)], W.at[d, c], loc.at[2]),
        pltpu.make_async_copy(wout.at[:, pl.ds(pl.multiple_of(u * 128, 128), 128)], WO.at[d], loc.at[3]),
        pltpu.make_async_copy(gain, GN.at[d], loc.at[4]),
    ]
    for cp in locals_:
        cp.start()

    def arrivals(a):
        own(a, 0, A, right).wait_recv()
        fwd(a, 4, left, A, right).start()
        relay(a, 0, left, A).start()
        own(a, 3, B, left).wait_recv()
        fwd(a, 5, right, B, left).start()
        relay(a, 3, right, B).start()

    def late(a):
        own(a, 1, B, right).wait_recv()
        relay(a, 1, left, B).start()
        own(a, 2, A, left).wait_recv()
        relay(a, 2, right, A).start()

    def last(a):
        fwd(a, 4, far, A, right).wait_recv()
        relay(a, 4, far, A).start()
        fwd(a, 5, far, B, left).wait_recv()
        relay(a, 5, far, B).start()

    arrivals(0)
    start_own(1)
    late(0)
    last(0)
    arrivals(1)

    for cp in locals_:
        cp.wait()

    @pl.loop(1, ND)
    def _(k):
        g_copy(k).wait()
        o_copy(k).wait()
        w_copy(k).wait()

    w_mate = remote(W.at[:, c], W.at[:, c], wps, wpr, mate, d)
    w_mate.start()
    late(1)
    last(1)
    w_mate.wait()
    for a in range(2):
        own(a, 0, A, right).wait_send()
        own(a, 1, B, right).wait_send()
        own(a, 2, A, left).wait_send()
        own(a, 3, B, left).wait_send()
        fwd(a, 4, left, A, right).wait_send()
        fwd(a, 5, right, B, left).wait_send()
        own_relay(a).wait()
        relay(a, 0, left, A).wait()
        relay(a, 1, left, B).wait()
        relay(a, 2, right, A).wait()
        relay(a, 3, right, B).wait()
        relay(a, 4, far, A).wait()
        relay(a, 5, far, B).wait()


def gather(tok, dout, wqkv, wout, gain):
    dma = pltpu.SemaphoreType.DMA
    hbm = pl.BlockSpec(memory_space=pl.ANY)
    vmem = pl.BlockSpec(memory_space=pltpu.VMEM)
    return pl.pallas_call(
        gather_kernel,
        name="gather",
        out_shape=(
            jax.ShapeDtypeStruct((NU, ROWS, D), BF16),
            jax.ShapeDtypeStruct((NU, ROWS, D), BF16),
            jax.ShapeDtypeStruct((ND, 2, 64, 1536), BF16),
            jax.ShapeDtypeStruct((ND, 128, 128), BF16),
            jax.ShapeDtypeStruct((ND, 8, 128), F32),
        ),
        in_specs=[vmem] * 5,
        out_specs=(hbm,) * 5,
        scratch_shapes=[
            dma((2, 6)), dma((2, 6)), dma((2, 7)), dma((2, 7)),
            dma((ND,)), dma((ND,)), dma((ND,)), dma((ND,)), dma((ND,)), dma((ND,)),
            dma, dma, dma((5,)),
        ],
        compiler_params=pltpu.CompilerParams(collective_id=0, has_side_effects=True),
    )(tok, dout, wqkv, wout, gain)


def rot_t(u, cos, sin):
    half = HEAD_DIM // 2
    return u * cos + jnp.concatenate([-u[half:], u[:half]], axis=0) * sin


def proj_kernel(tok, dout, wsel, wo, gain, cos, sin, normed, q_t, kv_t, kv, da_t):
    wide = tok[0].astype(F32)
    inv = lax.rsqrt(jnp.mean(wide * wide, axis=1, keepdims=True) + EPS)
    low = (wide * inv * gain[...]).astype(BF16)
    normed[...] = low
    proj_t = jnp.dot(low, wsel[...], preferred_element_type=F32).T
    cos_, sin_ = cos[...], sin[...]
    q_t[0:64, :] = rot_t(proj_t[0:64], cos_, sin_).astype(BF16)
    q_t[64:128, :] = rot_t(proj_t[64:128], cos_, sin_).astype(BF16)
    both = jnp.concatenate([rot_t(proj_t[128:192], cos_, sin_), proj_t[192:256]], axis=0)
    kv_t[...] = both.astype(BF16)
    kv[...] = both.T.astype(BF16)
    da_t[...] = jnp.dot(dout[0], wo[...], preferred_element_type=F32).T.astype(BF16)


def project(T, G, wsel, wo, gain, cos_t, sin_t):
    n = SEQ // ROWS
    col = pl.BlockSpec((128, ROWS), lambda i: (0, i))
    fixed = lambda shape: pl.BlockSpec(shape, lambda i: (0, 0))
    return pl.pallas_call(
        proj_kernel,
        name="project",
        grid=(n,),
        in_specs=[
            pl.BlockSpec((1, ROWS, D), lambda i: (i, 0, 0)),
            pl.BlockSpec((1, ROWS, D), lambda i: (i, 0, 0)),
            fixed((D, 256)), fixed((D, 128)), fixed((1, D)),
            pl.BlockSpec((64, ROWS), lambda i: (0, i)),
            pl.BlockSpec((64, ROWS), lambda i: (0, i)),
        ],
        out_specs=(
            pl.BlockSpec((ROWS, D), lambda i: (i, 0)),
            col, col, pl.BlockSpec((ROWS, 128), lambda i: (i, 0)), col,
        ),
        out_shape=(
            jax.ShapeDtypeStruct((SEQ, D), BF16),
            jax.ShapeDtypeStruct((128, SEQ), BF16),
            jax.ShapeDtypeStruct((128, SEQ), BF16),
            jax.ShapeDtypeStruct((SEQ, 128), BF16),
            jax.ShapeDtypeStruct((128, SEQ), BF16),
        ),
    )(T, G, wsel, wo, gain, cos_t, sin_t)


QB = 128
WIN = 512


def attend_kernel(q_t, da_t, begins, cos, sin, kv, kv_t, cos_all, sin_all, attn_t, dq_t, dkv_t, acc):
    i = pl.program_id(0)

    @pl.when(i == 0)
    def _():
        acc[...] = jnp.zeros_like(acc)

    start = pl.multiple_of(jnp.maximum(i - 3, 0) * QB, QB)
    keys = kv[pl.ds(start, WIN), :]
    keys_t = kv_t[:, pl.ds(start, WIN)]
    q = (q_t[...].astype(F32) * (HEAD_DIM ** -0.5)).astype(BF16)
    da = da_t[...]
    none = jnp.zeros((64, 2 * QB), BF16)
    q2 = jnp.concatenate([q[0:64], q[64:128]], axis=1)
    da2 = jnp.concatenate([da[0:64], da[64:128]], axis=1)
    mixed = jnp.concatenate(
        [jnp.concatenate([q2, none], axis=1), jnp.concatenate([none, da2], axis=1)], axis=0
    )
    st = jnp.dot(keys, mixed, preferred_element_type=F32)
    key_pos = start + lax.broadcasted_iota(jnp.int32, (WIN, QB), 0)
    query_pos = i * QB + lax.broadcasted_iota(jnp.int32, (WIN, QB), 1)
    allowed = (key_pos >= begins[...]) & (key_pos <= query_pos)
    s = jnp.concatenate(
        [jnp.where(allowed, st[:, 0:QB], -1e30), jnp.where(allowed, st[:, QB : 2 * QB], -1e30)], axis=1
    )
    w = jnp.exp(s - jnp.max(s, axis=0, keepdims=True))
    p = w * (1.0 / jnp.sum(w, axis=0, keepdims=True))
    pb = p.astype(BF16)
    o = jnp.dot(keys_t, pb, preferred_element_type=F32)[64:128]
    delta = jnp.sum(da2.astype(F32) * o, axis=0, keepdims=True)
    ds = (p * (st[:, 2 * QB :] - delta)).astype(BF16)
    dq = jnp.dot(keys_t, ds, preferred_element_type=F32)[0:64] * (HEAD_DIM ** -0.5)
    attn_t[0:64, :] = o[:, 0:QB].astype(BF16)
    attn_t[64:128, :] = o[:, QB:].astype(BF16)
    cos_, sin_ = cos[...], -sin[...]
    dq_t[0:64, :] = rot_t(dq[:, 0:QB], cos_, sin_).astype(BF16)
    dq_t[64:128, :] = rot_t(dq[:, QB:], cos_, sin_).astype(BF16)
    acc[pl.ds(start, WIN), :] += lax.dot_general(
        jnp.concatenate([ds, pb], axis=1), mixed, (((1,), (1,)), ((), ())), preferred_element_type=F32
    )

    @pl.when(i == pl.num_programs(0) - 1)
    def _():
        for b in range(SEQ // ROWS):
            cols = slice(b * ROWS, (b + 1) * ROWS)
            t = acc[b * ROWS : (b + 1) * ROWS, :].T
            dkv_t[0:64, cols] = rot_t(t[0:64], cos_all[:, cols], -sin_all[:, cols]).astype(BF16)
            dkv_t[64:128, cols] = t[64:128].astype(BF16)


def attend(q_t, da_t, begins, cos_t, sin_t, kv, kv_t):
    n = SEQ // QB
    col = lambda r: pl.BlockSpec((r, QB), lambda i: (0, i))
    fixed = lambda shape: pl.BlockSpec(shape, lambda i: (0, 0))
    return pl.pallas_call(
        attend_kernel,
        name="attend",
        grid=(n,),
        in_specs=[
            col(128), col(128), col(1), col(64), col(64),
            fixed((SEQ, 128)), fixed((128, SEQ)), fixed((64, SEQ)), fixed((64, SEQ)),
        ],
        out_specs=(col(128), col(128), fixed((128, SEQ))),
        out_shape=(jax.ShapeDtypeStruct((128, SEQ), BF16),) * 3,
        scratch_shapes=[pltpu.VMEM((SEQ, 128), F32)],
    )(q_t, da_t, begins, cos_t, sin_t, kv, kv_t, cos_t, sin_t)


def body(tokens, d_out, lengths, gain, w_qkv, w_out):
    u = lax.axis_index("ulysses")
    factor = 1.0 / math.sqrt(SEQ * ND)
    token_rows, grad_rows = tokens[0], d_out[0]
    gain_rep = jnp.broadcast_to(gain.astype(F32)[None, :], (8, 128))
    T, G, W, WO, GN = gather(token_rows, grad_rows, w_qkv, w_out, gain_rep)
    begins, places = doc_positions(lengths[0], SEQ)
    cos_t, sin_t = rotary_tables_t(places)
    gain_wide = GN[:, 0, :].reshape(1, D)
    w_full = W.reshape(D, QW + 2 * KW)
    kv_head = u // 2
    wsel = jnp.concatenate(
        [
            lax.dynamic_slice_in_dim(w_full, u * 128, 128, axis=1),
            lax.dynamic_slice_in_dim(w_full, QW + kv_head * 64, 64, axis=1),
            lax.dynamic_slice_in_dim(w_full, QW + KW + kv_head * 64, 64, axis=1),
        ],
        axis=1,
    )
    normed, q_t, kv_t, kv, da_t = project(T, G, wsel, WO.reshape(D, 128), gain_wide, cos_t, sin_t)
    attn_t, dq_t, dkv_t = attend(q_t, da_t, begins[None, :], cos_t, sin_t, kv, kv_t)

    other = lax.ppermute(dkv_t, "ulysses", [(i, i ^ 1) for i in range(NU)])
    dkv_t = (dkv_t.astype(F32) + other.astype(F32)).astype(BF16)
    mine_t = lax.dynamic_slice_in_dim(dkv_t, (u % 2) * 64, 64, axis=0)
    cols_t = jnp.concatenate([dq_t, mine_t], axis=0)
    back = cols_t.T.reshape(NU, ROWS, 192)
    back = lax.all_to_all(back, "ulysses", split_axis=0, concat_axis=0, tiled=True)
    dq_rows = back[:, :, :128].transpose(1, 0, 2).reshape(ROWS, QW)
    kv_rows = back[:, :, 128:].reshape(4, 2, ROWS, 64)
    dk_rows = kv_rows[:, 0].transpose(1, 0, 2).reshape(ROWS, KW)
    dv_rows = kv_rows[:, 1].transpose(1, 0, 2).reshape(ROWS, KW)
    d_proj = jnp.concatenate([dq_rows, dk_rows, dv_rows], axis=1)

    dw = jnp.concatenate(
        [
            jnp.einsum("ct,td->cd", cols_t, normed, preferred_element_type=F32),
            jnp.einsum("ct,td->cd", attn_t, G.reshape(SEQ, D), preferred_element_type=F32),
        ],
        axis=0,
    ).T
    dw = dw.reshape(NU, ND, 16, 320).transpose(1, 0, 2, 3).reshape(D, 320)
    dw = lax.psum_scatter(dw, "dp", scatter_dimension=0, tiled=True) * factor
    dw = lax.all_to_all(dw.reshape(NU, 16, 320), "ulysses", split_axis=0, concat_axis=0, tiled=True)
    gq = dw[:, :, 0:128].transpose(1, 0, 2).reshape(16, QW)
    gkv = dw[:, :, 128:192].reshape(4, 2, 16, 64)
    gk = gkv[:, 0].transpose(1, 0, 2).reshape(16, KW)
    gv = gkv[:, 1].transpose(1, 0, 2).reshape(16, KW)
    grad_out = dw[:, :, 192:].transpose(1, 0, 2).reshape(16, QW)
    grad_qkv = jnp.concatenate([gq, gk, gv], axis=1)

    wide = token_rows.astype(F32)
    inv = lax.rsqrt(jnp.mean(wide * wide, axis=1, keepdims=True) + EPS)
    unit = wide * inv
    d_normed = jnp.einsum("tc,dc->td", d_proj, w_full, preferred_element_type=F32)
    grad_gain = jnp.sum(d_normed * unit, axis=0) * factor
    scaled = d_normed * gain_wide
    d_rows = inv * (scaled - unit * jnp.mean(scaled * unit, axis=1, keepdims=True))
    d_tokens = (grad_rows.astype(F32) + d_rows).astype(BF16)
    grad_gain = lax.psum_scatter(grad_gain, ("ulysses", "dp"), scatter_dimension=0, tiled=True)
    return d_tokens[None], grad_qkv, grad_out, grad_gain


def solution(mesh):
    in_specs = (
        P("dp", "ulysses", None),
        P("dp", "ulysses", None),
        P("dp", None),
        P("dp"),
        P("dp", None),
        P("dp", None),
    )
    out_specs = (
        P("dp", "ulysses", None),
        P(("ulysses", "dp"), None),
        P(("ulysses", "dp"), None),
        P(("ulysses", "dp")),
    )
    return jax.shard_map(body, mesh=mesh, in_specs=in_specs, out_specs=out_specs, check_vma=False)
```

```python
import functools
import math

import jax
import jax.numpy as jnp
from jax import lax
from jax.experimental import pallas as pl
from jax.experimental.pallas import tpu as pltpu
from jax.sharding import PartitionSpec as P

HEADS = 16
KV_HEADS = 4
HEAD_DIM = 64
D = 2048
SEQ = 2048
ROWS = 256
QW = 1024
KW = 256
NU = 8
ND = 16
EPS = 1e-05
ROPE_BASE = 500000.0
MESH = pl.DeviceIdType.MESH
F32 = jnp.float32
BF16 = jnp.bfloat16


def doc_positions(doc_lengths, length):
    bounds = jnp.cumsum(doc_lengths) - doc_lengths
    places = jnp.arange(length, dtype=jnp.int32)
    begins = jnp.max(jnp.where(bounds[None, :] <= places[:, None], bounds[None, :], 0), axis=1)
    return begins, places - begins


def rotary_tables_t(places):
    inverse = ROPE_BASE ** (-jnp.arange(0, HEAD_DIM, 2).astype(F32) / HEAD_DIM)
    angles = inverse[:, None] * places.astype(F32)[None, :]
    cos, sin = jnp.cos(angles), jnp.sin(angles)
    return jnp.concatenate([cos, cos], axis=0), jnp.concatenate([sin, sin], axis=0)


def remote(src, dst, send_sem, recv_sem, u, d):
    return pltpu.make_async_remote_copy(
        src_ref=src, dst_ref=dst, send_sem=send_sem, recv_sem=recv_sem,
        device_id={"ulysses": u, "dp": d}, device_id_type=MESH,
    )


def gather_kernel(tok, dout, wqkv, wout, gain, T, G, W, WO, GN,
                  zs, zr, ps, pr, ws, wr, os_, or_, gs, gr, wps, wpr, loc):
    u = lax.axis_index("ulysses")
    d = lax.axis_index("dp")
    z, c = u // 2, u % 2
    right = ((z + 1) % 4) * 2 + c
    left = ((z + 3) % 4) * 2 + c
    far = ((z + 2) % 4) * 2 + c
    mate = z * 2 + (1 - c)

    barrier = pltpu.get_barrier_semaphore()
    for peer in (right, left, mate):
        pl.semaphore_signal(barrier, inc=1, device_id={"ulysses": peer, "dp": d}, device_id_type=MESH)

    @pl.loop(1, ND)
    def _(k):
        pl.semaphore_signal(barrier, inc=1, device_id={"ulysses": u, "dp": (d + k) % ND}, device_id_type=MESH)

    pl.semaphore_wait(barrier, 3 + ND - 1)

    H = ROWS // 2
    A, B = pl.ds(0, H), pl.ds(H, H)
    srcs, dsts = (tok, dout), (T, G)

    def own(a, slot, rows, to):
        return remote(srcs[a].at[rows], dsts[a].at[u, rows], zs.at[a, slot], zr.at[a, slot], to, d)

    def fwd(a, slot, frm, rows, to):
        return remote(dsts[a].at[frm, rows], dsts[a].at[frm, rows], zs.at[a, slot], zr.at[a, slot], to, d)

    def relay(a, slot, frm, rows):
        return remote(dsts[a].at[frm, rows], dsts[a].at[frm, rows], ps.at[a, slot], pr.at[a, slot], mate, d)

    def own_relay(a):
        return remote(srcs[a], dsts[a].at[u], ps.at[a, 6], pr.at[a, 6], mate, d)

    def start_own(a):
        own(a, 0, A, right).start()
        own(a, 3, B, left).start()
        own(a, 1, B, right).start()
        own(a, 2, A, left).start()
        own_relay(a).start()

    start_own(0)

    HW = wqkv.shape[0] // 2

    def w_copy(k):
        to = (d + k) % ND
        return remote(wqkv.at[pl.ds(c * HW, HW)], W.at[d, c], ws.at[k], wr.at[k], u, to)

    def o_copy(k):
        to = (d + k) % ND
        return remote(wout.at[:, pl.ds(pl.multiple_of(u * 128, 128), 128)], WO.at[d], os_.at[k], or_.at[k], u, to)

    def g_copy(k):
        to = (d + k) % ND
        return remote(gain, GN.at[d], gs.at[k], gr.at[k], u, to)

    @pl.loop(1, ND)
    def _(k):
        g_copy(k).start()
        o_copy(k).start()
        w_copy(k).start()

    locals_ = [
        pltpu.make_async_copy(tok, T.at[u], loc.at[0]),
        pltpu.make_async_copy(dout, G.at[u], loc.at[1]),
        pltpu.make_async_copy(wqkv.at[pl.ds(c * HW, HW)], W.at[d, c], loc.at[2]),
        pltpu.make_async_copy(wout.at[:, pl.ds(pl.multiple_of(u * 128, 128), 128)], WO.at[d], loc.at[3]),
        pltpu.make_async_copy(gain, GN.at[d], loc.at[4]),
    ]
    for cp in locals_:
        cp.start()

    def arrivals(a):
        own(a, 0, A, right).wait_recv()
        fwd(a, 4, left, A, right).start()
        relay(a, 0, left, A).start()
        own(a, 3, B, left).wait_recv()
        fwd(a, 5, right, B, left).start()
        relay(a, 3, right, B).start()

    def late(a):
        own(a, 1, B, right).wait_recv()
        relay(a, 1, left, B).start()
        own(a, 2, A, left).wait_recv()
        relay(a, 2, right, A).start()

    def last(a):
        fwd(a, 4, far, A, right).wait_recv()
        relay(a, 4, far, A).start()
        fwd(a, 5, far, B, left).wait_recv()
        relay(a, 5, far, B).start()

    arrivals(0)
    start_own(1)
    late(0)
    last(0)
    arrivals(1)

    for cp in locals_:
        cp.wait()

    @pl.loop(1, ND)
    def _(k):
        g_copy(k).wait()
        o_copy(k).wait()
        w_copy(k).wait()

    w_mate = remote(W.at[:, c], W.at[:, c], wps, wpr, mate, d)
    w_mate.start()
    late(1)
    last(1)
    w_mate.wait()
    for a in range(2):
        own(a, 0, A, right).wait_send()
        own(a, 1, B, right).wait_send()
        own(a, 2, A, left).wait_send()
        own(a, 3, B, left).wait_send()
        fwd(a, 4, left, A, right).wait_send()
        fwd(a, 5, right, B, left).wait_send()
        own_relay(a).wait()
        relay(a, 0, left, A).wait()
        relay(a, 1, left, B).wait()
        relay(a, 2, right, A).wait()
        relay(a, 3, right, B).wait()
        relay(a, 4, far, A).wait()
        relay(a, 5, far, B).wait()


def gather(tok, dout, wqkv, wout, gain):
    dma = pltpu.SemaphoreType.DMA
    hbm = pl.BlockSpec(memory_space=pl.ANY)
    vmem = pl.BlockSpec(memory_space=pltpu.VMEM)
    return pl.pallas_call(
        gather_kernel,
        name="gather",
        out_shape=(
            jax.ShapeDtypeStruct((NU, ROWS, D), BF16),
            jax.ShapeDtypeStruct((NU, ROWS, D), BF16),
            jax.ShapeDtypeStruct((ND, 2, 64, 1536), BF16),
            jax.ShapeDtypeStruct((ND, 128, 128), BF16),
            jax.ShapeDtypeStruct((ND, 8, 128), F32),
        ),
        in_specs=[vmem] * 5,
        out_specs=(hbm,) * 5,
        scratch_shapes=[
            dma((2, 6)), dma((2, 6)), dma((2, 7)), dma((2, 7)),
            dma((ND,)), dma((ND,)), dma((ND,)), dma((ND,)), dma((ND,)), dma((ND,)),
            dma, dma, dma((5,)),
        ],
        compiler_params=pltpu.CompilerParams(collective_id=0, has_side_effects=True),
    )(tok, dout, wqkv, wout, gain)


def rot_t(u, cos, sin):
    half = HEAD_DIM // 2
    return u * cos + jnp.concatenate([-u[half:], u[:half]], axis=0) * sin


def proj_kernel(tok, dout, wsel, wo, gain, cos, sin, normed, q_t, kv_t, kv, da_t):
    wide = tok[0].astype(F32)
    inv = lax.rsqrt(jnp.mean(wide * wide, axis=1, keepdims=True) + EPS)
    low = (wide * inv * gain[...]).astype(BF16)
    normed[...] = low
    proj_t = jnp.dot(low, wsel[...], preferred_element_type=F32).T
    cos_, sin_ = cos[...], sin[...]
    q_t[0:64, :] = rot_t(proj_t[0:64], cos_, sin_).astype(BF16)
    q_t[64:128, :] = rot_t(proj_t[64:128], cos_, sin_).astype(BF16)
    both = jnp.concatenate([rot_t(proj_t[128:192], cos_, sin_), proj_t[192:256]], axis=0)
    kv_t[...] = both.astype(BF16)
    kv[...] = both.T.astype(BF16)
    da_t[...] = jnp.dot(dout[0], wo[...], preferred_element_type=F32).T.astype(BF16)


def project(T, G, wsel, wo, gain, cos_t, sin_t):
    n = SEQ // ROWS
    col = pl.BlockSpec((128, ROWS), lambda i: (0, i))
    fixed = lambda shape: pl.BlockSpec(shape, lambda i: (0, 0))
    return pl.pallas_call(
        proj_kernel,
        name="project",
        grid=(n,),
        in_specs=[
            pl.BlockSpec((1, ROWS, D), lambda i: (i, 0, 0)),
            pl.BlockSpec((1, ROWS, D), lambda i: (i, 0, 0)),
            fixed((D, 256)), fixed((D, 128)), fixed((1, D)),
            pl.BlockSpec((64, ROWS), lambda i: (0, i)),
            pl.BlockSpec((64, ROWS), lambda i: (0, i)),
        ],
        out_specs=(
            pl.BlockSpec((ROWS, D), lambda i: (i, 0)),
            col, col, pl.BlockSpec((ROWS, 128), lambda i: (i, 0)), col,
        ),
        out_shape=(
            jax.ShapeDtypeStruct((SEQ, D), BF16),
            jax.ShapeDtypeStruct((128, SEQ), BF16),
            jax.ShapeDtypeStruct((128, SEQ), BF16),
            jax.ShapeDtypeStruct((SEQ, 128), BF16),
            jax.ShapeDtypeStruct((128, SEQ), BF16),
        ),
    )(T, G, wsel, wo, gain, cos_t, sin_t)


QB = 128
WIN = 512


def attend_kernel(q_t, da_t, begins, cos, sin, kv, kv_t, cos_all, sin_all, attn_t, dq_t, dq_n, dkv, acc):
    i = pl.program_id(0)

    @pl.when(i == 0)
    def _():
        acc[...] = jnp.zeros_like(acc)

    start = pl.multiple_of(jnp.maximum(i - 3, 0) * QB, QB)
    keys = kv[pl.ds(start, WIN), :]
    keys_t = kv_t[:, pl.ds(start, WIN)]
    q = (q_t[...].astype(F32) * (HEAD_DIM ** -0.5)).astype(BF16)
    da = da_t[...]
    none = jnp.zeros((64, 2 * QB), BF16)
    q2 = jnp.concatenate([q[0:64], q[64:128]], axis=1)
    da2 = jnp.concatenate([da[0:64], da[64:128]], axis=1)
    mixed = jnp.concatenate(
        [jnp.concatenate([q2, none], axis=1), jnp.concatenate([none, da2], axis=1)], axis=0
    )
    st = jnp.dot(keys, mixed, preferred_element_type=F32)
    key_pos = start + lax.broadcasted_iota(jnp.int32, (WIN, QB), 0)
    query_pos = i * QB + lax.broadcasted_iota(jnp.int32, (WIN, QB), 1)
    allowed = (key_pos >= begins[...]) & (key_pos <= query_pos)
    s = jnp.concatenate(
        [jnp.where(allowed, st[:, 0:QB], -1e30), jnp.where(allowed, st[:, QB : 2 * QB], -1e30)], axis=1
    )
    w = jnp.exp(s - jnp.max(s, axis=0, keepdims=True))
    p = w * (1.0 / jnp.sum(w, axis=0, keepdims=True))
    pb = p.astype(BF16)
    o = jnp.dot(keys_t, pb, preferred_element_type=F32)[64:128]
    delta = jnp.sum(da2.astype(F32) * o, axis=0, keepdims=True)
    ds = (p * (st[:, 2 * QB :] - delta)).astype(BF16)
    dq = jnp.dot(keys_t, ds, preferred_element_type=F32)[0:64] * (HEAD_DIM ** -0.5)
    attn_t[0:64, :] = o[:, 0:QB].astype(BF16)
    attn_t[64:128, :] = o[:, QB:].astype(BF16)
    cos_, sin_ = cos[...], -sin[...]
    turned = jnp.concatenate([rot_t(dq[:, 0:QB], cos_, sin_), rot_t(dq[:, QB:], cos_, sin_)], axis=0)
    dq_t[...] = turned.astype(BF16)
    dq_n[...] = turned.T.astype(BF16)
    acc[pl.ds(start, WIN), :] += lax.dot_general(
        jnp.concatenate([ds, pb], axis=1), mixed, (((1,), (1,)), ((), ())), preferred_element_type=F32
    )

    @pl.when(i == pl.num_programs(0) - 1)
    def _():
        for b in range(SEQ // ROWS):
            cols = slice(b * ROWS, (b + 1) * ROWS)
            t = acc[cols, :].T
            t = jnp.concatenate([rot_t(t[0:64], cos_all[:, cols], -sin_all[:, cols]), t[64:128]], axis=0)
            dkv[cols, :] = t.T.astype(BF16)


def attend(q_t, da_t, begins, cos_t, sin_t, kv, kv_t):
    n = SEQ // QB
    col = lambda r: pl.BlockSpec((r, QB), lambda i: (0, i))
    fixed = lambda shape: pl.BlockSpec(shape, lambda i: (0, 0))
    return pl.pallas_call(
        attend_kernel,
        name="attend",
        grid=(n,),
        in_specs=[
            col(128), col(128), col(1), col(64), col(64),
            fixed((SEQ, 128)), fixed((128, SEQ)), fixed((64, SEQ)), fixed((64, SEQ)),
        ],
        out_specs=(col(128), col(128), pl.BlockSpec((QB, 128), lambda i: (i, 0)), fixed((SEQ, 128))),
        out_shape=(jax.ShapeDtypeStruct((128, SEQ), BF16),) * 2 + (jax.ShapeDtypeStruct((SEQ, 128), BF16),) * 2,
        scratch_shapes=[pltpu.VMEM((SEQ, 128), F32)],
    )(q_t, da_t, begins, cos_t, sin_t, kv, kv_t, cos_t, sin_t)


FACTOR = 1.0 / math.sqrt(SEQ * ND)
HALF = 80
PART = 40


def finish_kernel(dq_t, attn_t, dq, dkv, tok, dout, gain, normed_h, g_h, w_h,
                  dtok_o, gqkv_o, gout_o, ggain_o,
                  N, GG, W, DP, RKV, OT, KVS, KVT, R, B1, B2, FIN, FKV, DN, gbuf, GR, gsum, GU,
                  load, ms, mr, qs, qr, ks, kr, rs, rr, fs, fr, vs, vr, gs, gr, us, ur):
    u = lax.axis_index("ulysses")
    d = lax.axis_index("dp")
    z, c = u // 2, u % 2
    x, y = d // 4, d % 4
    mate = z * 2 + (1 - c)

    def n_load(f):
        cols = pl.ds(pl.multiple_of(f * 256, 256), 256)
        return pltpu.make_async_copy(normed_h.at[:, cols], N.at[f], load.at[0, f])

    def g_load(f):
        cols = pl.ds(pl.multiple_of(f * 256, 256), 256)
        return pltpu.make_async_copy(g_h.at[:, cols], GG.at[f], load.at[1, f])

    w_load = pltpu.make_async_copy(w_h, W, load.at[2, 0])

    @pl.loop(0, NU)
    def _(f):
        n_load(f).start()
        g_load(f).start()

    w_load.start()

    barrier = pltpu.get_barrier_semaphore()

    @pl.loop(1, NU)
    def _(k):
        pl.semaphore_signal(barrier, inc=1, device_id={"ulysses": (u + k) % NU, "dp": d}, device_id_type=MESH)

    @pl.loop(1, ND)
    def _(k):
        pl.semaphore_signal(barrier, inc=1, device_id={"ulysses": u, "dp": (d + k) % ND}, device_id_type=MESH)

    pl.semaphore_wait(barrier, NU + ND - 2)

    def q_copy(k):
        to = (u + k) % NU
        rows = pl.ds(pl.multiple_of(to * ROWS, ROWS), ROWS)
        cols = pl.ds(pl.multiple_of(u * 128, 128), 128)
        return remote(dq.at[rows], DP.at[:, cols], qs.at[k], qr.at[k], to, d)

    def kv_copy(k):
        to = (u + k) % NU
        rows = pl.ds(pl.multiple_of(to * ROWS + c * 128, 128), 128)
        return remote(KVS.at[rows], RKV.at[z, pl.ds(pl.multiple_of(c * 128, 128), 128)], ks.at[k], kr.at[k], to, d)

    m_copy = remote(dkv, OT, ms, mr, mate, d)
    m_copy.start()

    @pl.loop(1, NU)
    def _(k):
        q_copy(k).start()

    DP[:, pl.ds(pl.multiple_of(u * 128, 128), 128)] = dq[pl.ds(pl.multiple_of(u * ROWS, ROWS), ROWS), :]

    def dw_block(f):
        n_load(f).wait()
        g_load(f).wait()
        rows = pl.ds(pl.multiple_of(f * 16, 16), 16)
        q = jnp.dot(dq_t[...], N[f], preferred_element_type=F32)
        R[:, :, rows, 0:128] = q.T.reshape(4, 4, 16, 128)
        o = jnp.dot(attn_t[...], GG[f], preferred_element_type=F32)
        R[:, :, rows, 128:256] = o.T.reshape(4, 4, 16, 128)

    dw_block(0)

    m_copy.wait()

    @pl.loop(0, NU)
    def _(b):
        rows = pl.ds(pl.multiple_of(b * ROWS, ROWS), ROWS)
        both = (dkv[rows, :].astype(F32) + OT[rows, :].astype(F32)).astype(BF16)
        KVS[rows, :] = both
        KVT[:, rows] = both.astype(F32).T.astype(BF16)

    @pl.loop(1, NU)
    def _(k):
        kv_copy(k).start()

    RKV[z, pl.ds(pl.multiple_of(c * 128, 128), 128), :] = KVS[
        pl.ds(pl.multiple_of(u * ROWS + c * 128, 128), 128), :
    ]

    @pl.loop(1, 5)
    def _(f):
        dw_block(f)

    def along_x(h, st):
        return (h == 0) == (st == 0)

    def near(h, st, step):
        if along_x(h, st):
            return ((x + step) % 4) * 4 + y
        return x * 4 + (y + step) % 4

    def piece(h, st, step, part):
        rows = pl.ds(h * HALF + part * PART, PART)
        if along_x(h, st):
            j = (x + step) % 4
            return R.at[j, :, rows, :] if st == 0 else R.at[j, y, rows, :]
        j = (y + step) % 4
        return R.at[:, j, rows, :] if st == 0 else R.at[x, j, rows, :]

    def buf(h, st, slot):
        return B1.at[h, slot] if st == 0 else B2.at[h, slot]

    ROUTE = ((2, 0, 1), (2, 1, 3), (1, 1, 1), (3, 0, 3), (1, 0, 1), (3, 1, 3))

    def rcp(h, st, slot):
        step, part, to = ROUTE[slot]
        return remote(piece(h, st, step, part), buf(h, st, slot), rs.at[h, st, slot], rr.at[h, st, slot],
                      u, near(h, st, to))

    def start(h, st):
        for slot in range(4):
            rcp(h, st, slot).start()

    def pass_on(h, st):
        for slot, step, part in ((0, 1, 0), (1, 3, 1)):
            rcp(h, st, slot).wait_recv()
            p = piece(h, st, step, part)
            p[...] = p[...] + buf(h, st, slot)[...]
            rcp(h, st, slot + 4).start()

    def gather_up(h, st):
        for part, one, two in ((0, 3, 4), (1, 2, 5)):
            rcp(h, st, one).wait_recv()
            rcp(h, st, two).wait_recv()
            p = piece(h, st, 0, part)
            p[...] = p[...] + (buf(h, st, one)[...] + buf(h, st, two)[...])

    start(0, 0)

    @pl.loop(5, NU)
    def _(f):
        dw_block(f)

    for i in range(4):
        kvp = jnp.dot(KVT[...], N[c * 4 + i], preferred_element_type=F32)
        R[:, :, 128 + (i // 2) * 16 : 144 + (i // 2) * 16, (i % 2) * 128 : (i % 2) * 128 + 128] = (
            kvp.T.reshape(4, 4, 16, 128)
        )

    start(1, 0)
    pass_on(0, 0)
    pass_on(1, 0)

    @pl.loop(1, NU)
    def _(k):
        q_copy(k).wait()
        kv_copy(k).wait()

    w_load.wait()
    for i in range(2):
        a, b = RKV[2 * i], RKV[2 * i + 1]
        DP[:, QW + i * 128 : QW + (i + 1) * 128] = jnp.concatenate([a[:, 0:64], b[:, 0:64]], axis=1)
        DP[:, QW + KW + i * 128 : QW + KW + (i + 1) * 128] = jnp.concatenate([a[:, 64:], b[:, 64:]], axis=1)

    wide = tok[...].astype(F32)
    inv = lax.rsqrt(jnp.mean(wide * wide, axis=1, keepdims=True) + EPS)

    def back(f, along):
        cols = pl.ds(pl.multiple_of(f * 256, 256), 256)
        dn = lax.dot_general(DP[...], W[cols, :], (((1,), (1,)), ((), ())), preferred_element_type=F32)
        unit = tok[:, cols].astype(F32) * inv
        gbuf[pl.ds(f, 1), :] = jnp.sum(dn * unit, axis=0, keepdims=True)
        scaled = dn * gain[:, cols]
        DN[f] = scaled
        return along + jnp.sum(scaled * unit, axis=1, keepdims=True)

    along = lax.fori_loop(0, NU, back, jnp.zeros((ROWS, 1), F32))
    mean = along * (1.0 / D)

    def g_copy(k):
        return remote(gbuf, GR.at[d], gs.at[k], gr.at[k], u, (d + k) % ND)

    @pl.loop(1, ND)
    def _(k):
        g_copy(k).start()

    GR[d] = gbuf[...]

    gather_up(0, 0)
    start(0, 1)
    gather_up(1, 0)
    start(1, 1)

    @pl.loop(0, NU)
    def _(f):
        cols = pl.ds(pl.multiple_of(f * 256, 256), 256)
        unit = tok[:, cols].astype(F32) * inv
        d_rows = inv * (DN[f] - unit * mean)
        dtok_o[:, cols] = (dout[:, cols].astype(F32) + d_rows).astype(BF16)

    pass_on(0, 1)
    pass_on(1, 1)

    @pl.loop(1, ND)
    def _(k):
        g_copy(k).wait()

    gsum[...] = jnp.sum(GR[...], axis=0)

    def gu_copy(k):
        return remote(gsum, GU.at[u], us.at[k], ur.at[k], (u + k) % NU, d)

    @pl.loop(1, NU)
    def _(k):
        gu_copy(k).start()

    GU[u] = gsum[...]
    gather_up(0, 1)
    gather_up(1, 1)

    def f_copy(k):
        to = (u + k) % NU
        return remote(R.at[x, y, pl.ds(pl.multiple_of(to * 16, 16), 16)], FIN.at[u], fs.at[k], fr.at[k], to, d)

    @pl.loop(1, NU)
    def _(k):
        f_copy(k).start()

    def v_block(i):
        return R.at[x, y, pl.ds(128 + (i // 2) * 16, 16), pl.ds((i % 2) * 128, 128)]

    def v_copy(i):
        return remote(v_block(i), FKV.at[z], vs.at[i], vr.at[z], c * 4 + i, d)

    def v_arrival(zs):
        return remote(v_block(0), FKV.at[zs], vs.at[0], vr.at[zs], u, d)

    for i in range(4):
        @pl.when(c * 4 + i != u)
        def _():
            v_copy(i).start()

        @pl.when(c * 4 + i == u)
        def _():
            FKV[z] = v_block(i)[...]

    FIN[u] = R[x, y, pl.ds(pl.multiple_of(u * 16, 16), 16), :]

    @pl.loop(1, NU)
    def _(k):
        gu_copy(k).wait()

    ggain_o[...] = jnp.sum(GU[...], axis=0) * FACTOR

    @pl.loop(1, NU)
    def _(k):
        f_copy(k).wait()

    for i in range(4):
        @pl.when(i * 2 + u // 4 != u)
        def _():
            v_arrival(i).wait_recv()

        @pl.when(c * 4 + i != u)
        def _():
            v_copy(i).wait_send()

    for i in range(NU):
        gqkv_o[:, i * 128 : (i + 1) * 128] = FIN[i, :, 0:128] * FACTOR
        gout_o[:, i * 128 : (i + 1) * 128] = FIN[i, :, 128:256] * FACTOR
    for i in range(2):
        a, b = FKV[2 * i] * FACTOR, FKV[2 * i + 1] * FACTOR
        gqkv_o[:, QW + i * 128 : QW + (i + 1) * 128] = jnp.concatenate([a[:, 0:64], b[:, 0:64]], axis=1)
        gqkv_o[:, QW + KW + i * 128 : QW + KW + (i + 1) * 128] = jnp.concatenate([a[:, 64:], b[:, 64:]], axis=1)

    for h in range(2):
        for st in range(2):
            for slot in range(6):
                rcp(h, st, slot).wait_send()


def finish(dq_t, attn_t, dq, dkv, tok, dout, gain, normed, g, w):
    dma = pltpu.SemaphoreType.DMA
    hbm = pl.BlockSpec(memory_space=pl.ANY)
    vmem = pl.BlockSpec(memory_space=pltpu.VMEM)
    V = pltpu.VMEM
    return pl.pallas_call(
        finish_kernel,
        name="finish",
        out_shape=(
            jax.ShapeDtypeStruct((ROWS, D), BF16),
            jax.ShapeDtypeStruct((16, QW + 2 * KW), F32),
            jax.ShapeDtypeStruct((16, QW), F32),
            jax.ShapeDtypeStruct((NU, 256), F32),
        ),
        in_specs=[vmem] * 7 + [hbm] * 3,
        out_specs=(vmem,) * 4,
        scratch_shapes=[
            V((NU, SEQ, 256), BF16), V((NU, SEQ, 256), BF16), V((D, QW + 2 * KW), BF16),
            V((ROWS, QW + 2 * KW), BF16), V((4, ROWS, 128), BF16),
            V((SEQ, 128), BF16), V((SEQ, 128), BF16), V((128, SEQ), BF16),
            V((4, 4, 2 * HALF, 256), F32), V((2, 6, 4, PART, 256), F32), V((2, 6, PART, 256), F32),
            V((NU, 16, 256), F32), V((4, 16, 128), F32), V((NU, ROWS, 256), F32),
            V((NU, 256), F32), V((ND, NU, 256), F32), V((NU, 256), F32), V((NU, NU, 256), F32),
            dma((3, NU)), dma, dma, dma((NU,)), dma((NU,)), dma((NU,)), dma((NU,)),
            dma((2, 2, 6)), dma((2, 2, 6)), dma((NU,)), dma((NU,)), dma((4,)), dma((4,)),
            dma((ND,)), dma((ND,)), dma((NU,)), dma((NU,)),
        ],
        compiler_params=pltpu.CompilerParams(
            collective_id=1, has_side_effects=True, vmem_limit_bytes=60 * 1024 * 1024
        ),
    )(dq_t, attn_t, dq, dkv, tok, dout, gain, normed, g, w)


def body(tokens, d_out, lengths, gain, w_qkv, w_out):
    u = lax.axis_index("ulysses")
    d = lax.axis_index("dp")
    token_rows, grad_rows = tokens[0], d_out[0]
    gain_rep = jnp.broadcast_to(gain.astype(F32)[None, :], (8, 128))
    T, G, W, WO, GN = gather(token_rows, grad_rows, w_qkv, w_out, gain_rep)
    begins, places = doc_positions(lengths[0], SEQ)
    cos_t, sin_t = rotary_tables_t(places)
    gain_wide = GN[:, 0, :].reshape(1, D)
    w_full = W.reshape(D, QW + 2 * KW)
    kv_head = u // 2
    wsel = jnp.concatenate(
        [
            lax.dynamic_slice_in_dim(w_full, u * 128, 128, axis=1),
            lax.dynamic_slice_in_dim(w_full, QW + kv_head * 64, 64, axis=1),
            lax.dynamic_slice_in_dim(w_full, QW + KW + kv_head * 64, 64, axis=1),
        ],
        axis=1,
    )
    normed, q_t, kv_t, kv, da_t = project(T, G, wsel, WO.reshape(D, 128), gain_wide, cos_t, sin_t)
    attn_t, dq_t, dq, dkv = attend(q_t, da_t, begins[None, :], cos_t, sin_t, kv, kv_t)
    d_tokens, grad_qkv, grad_out, gain_sum = finish(
        dq_t, attn_t, dq, dkv, token_rows, grad_rows, gain_wide, normed, G.reshape(SEQ, D), w_full
    )
    grad_gain = lax.dynamic_slice(gain_sum, (u, d * 16), (1, 16)).reshape(16)
    return d_tokens[None], grad_qkv, grad_out, grad_gain


def solution(mesh):
    in_specs = (
        P("dp", "ulysses", None),
        P("dp", "ulysses", None),
        P("dp", None),
        P("dp"),
        P("dp", None),
        P("dp", None),
    )
    out_specs = (
        P("dp", "ulysses", None),
        P(("ulysses", "dp"), None),
        P(("ulysses", "dp"), None),
        P(("ulysses", "dp")),
    )
    return jax.shard_map(body, mesh=mesh, in_specs=in_specs, out_specs=out_specs, check_vma=False)
```

```python
import math

import jax
import jax.numpy as jnp
from jax import lax
from jax.experimental import pallas as pl
from jax.experimental.pallas import tpu as pltpu
from jax.sharding import PartitionSpec as P

HEADS = 16
KV_HEADS = 4
HEAD_DIM = 64
D = 2048
SEQ = 2048
ROWS = 256
QW = 1024
KW = 256
NU = 8
ND = 16
EPS = 1e-05
ROPE_BASE = 500000.0
MESH = pl.DeviceIdType.MESH
F32 = jnp.float32
BF16 = jnp.bfloat16


def doc_positions(doc_lengths, length):
    bounds = jnp.cumsum(doc_lengths) - doc_lengths
    places = jnp.arange(length, dtype=jnp.int32)
    begins = jnp.max(jnp.where(bounds[None, :] <= places[:, None], bounds[None, :], 0), axis=1)
    return begins, places - begins


def rotary_tables_t(places):
    inverse = ROPE_BASE ** (-jnp.arange(0, HEAD_DIM, 2).astype(F32) / HEAD_DIM)
    angles = inverse[:, None] * places.astype(F32)[None, :]
    cos, sin = jnp.cos(angles), jnp.sin(angles)
    return jnp.concatenate([cos, cos], axis=0), jnp.concatenate([sin, sin], axis=0)


def remote(src, dst, send_sem, recv_sem, u, d):
    return pltpu.make_async_remote_copy(
        src_ref=src, dst_ref=dst, send_sem=send_sem, recv_sem=recv_sem,
        device_id={"ulysses": u, "dp": d}, device_id_type=MESH,
    )


QB = 128
WIN = 512
FACTOR = 1.0 / math.sqrt(SEQ * ND)
HALF = 80
PART = 40


def rot_t(u, cos, sin):
    half = HEAD_DIM // 2
    return u * cos + jnp.concatenate([-u[half:], u[:half]], axis=0) * sin


def step_kernel(tok, dout, begins, cos, sin, gain_in, wqkv, wout,
                dtok_o, gqkv_o, gout_o, ggain_o,
                T, N, G, W, WO, GN, gain_rows, gain, WS, q_t, kv_t, kv, da_t, attn_t, dq_t, dq, dkv, acc,
                DP, RKV, OT, KVS, KVT, R, B1, B2, FIN, FKV, DN, gbuf, GR, gsum, GU,
                zs, zr, ps, pr, ws, wr, os_, or_, gns, gnr, wps, wpr, loc,
                ms, mr, qs, qr, ks, kr, rs, rr, fs, fr, vs, vr, gs, gr, us, ur):
    u = lax.axis_index("ulysses")
    d = lax.axis_index("dp")
    z, c = u // 2, u % 2
    x, y = d // 4, d % 4
    right = ((z + 1) % 4) * 2 + c
    left = ((z + 3) % 4) * 2 + c
    far = ((z + 2) % 4) * 2 + c
    mate = z * 2 + (1 - c)

    gain_rows[...] = jnp.broadcast_to(gain_in[...].astype(F32), (8, 128))
    barrier = pltpu.get_barrier_semaphore()

    @pl.loop(1, NU)
    def _(k):
        pl.semaphore_signal(barrier, inc=1, device_id={"ulysses": (u + k) % NU, "dp": d}, device_id_type=MESH)

    @pl.loop(1, ND)
    def _(k):
        pl.semaphore_signal(barrier, inc=1, device_id={"ulysses": u, "dp": (d + k) % ND}, device_id_type=MESH)

    pl.semaphore_wait(barrier, NU + ND - 2)

    H = ROWS // 2
    A, B = pl.ds(0, H), pl.ds(H, H)
    srcs, dsts = (tok, dout), (T, G)

    def own(a, slot, rows, to):
        return remote(srcs[a].at[rows], dsts[a].at[u, rows], zs.at[a, slot], zr.at[a, slot], to, d)

    def fwd(a, slot, frm, rows, to):
        return remote(dsts[a].at[frm, rows], dsts[a].at[frm, rows], zs.at[a, slot], zr.at[a, slot], to, d)

    def relay(a, slot, frm, rows):
        return remote(dsts[a].at[frm, rows], dsts[a].at[frm, rows], ps.at[a, slot], pr.at[a, slot], mate, d)

    def own_relay(a):
        return remote(srcs[a], dsts[a].at[u], ps.at[a, 6], pr.at[a, 6], mate, d)

    def start_own(a):
        own(a, 0, A, right).start()
        own(a, 3, B, left).start()
        own(a, 1, B, right).start()
        own(a, 2, A, left).start()
        own_relay(a).start()

    start_own(0)

    def along_x(h, st):
        return (h == 0) == (st == 0)

    def near(h, st, step):
        if along_x(h, st):
            return ((x + step) % 4) * 4 + y
        return x * 4 + (y + step) % 4

    def w_piece(h, st, step, part):
        rows = pl.ds(h * 32 + part * 16, 16)
        if along_x(h, st):
            j = (x + step) % 4
            return W.at[j, y, c, rows] if st == 0 else W.at[j, :, c, rows]
        j = (y + step) % 4
        return W.at[x, j, c, rows] if st == 0 else W.at[:, j, c, rows]

    W_ROUTE = ((0, 0, 1), (0, 1, 3), (0, 1, 1), (0, 0, 3), (3, 0, 1), (1, 1, 3))

    def w_copy(h, st, slot):
        step, part, to = W_ROUTE[slot]
        if st == 0 and step == 0:
            src = wqkv.at[pl.ds(c * 64 + h * 32 + part * 16, 16)]
        else:
            src = w_piece(h, st, step, part)
        return remote(src, w_piece(h, st, step, part), ws.at[h, st, slot], wr.at[h, st, slot], u, near(h, st, to))

    def w_start(h, st):
        for slot in range(4):
            w_copy(h, st, slot).start()

    def w_pass(h, st):
        for slot in range(2):
            w_copy(h, st, slot).wait_recv()
            w_copy(h, st, slot + 4).start()

    def w_end(h, st):
        for slot in range(2, 6):
            w_copy(h, st, slot).wait_recv()

    def o_copy(k):
        to = (d + k) % ND
        return remote(wout.at[:, pl.ds(pl.multiple_of(u * 128, 128), 128)], WO.at[d], os_.at[k], or_.at[k], u, to)

    def gain_copy(k):
        to = (d + k) % ND
        return remote(gain_rows, GN.at[d], gns.at[k], gnr.at[k], u, to)

    w_local = pltpu.make_async_copy(wqkv.at[pl.ds(c * 64, 64)], W.at[x, y, c], loc)
    w_local.start()
    w_start(0, 0)
    w_start(1, 0)

    @pl.loop(1, ND)
    def _(k):
        gain_copy(k).start()

    T[u] = tok[...]
    G[u] = dout[...]
    GN[d] = gain_rows[...]
    WO[d] = wout[:, pl.ds(pl.multiple_of(u * 128, 128), 128)]

    def arrivals(a):
        own(a, 0, A, right).wait_recv()
        fwd(a, 4, left, A, right).start()
        relay(a, 0, left, A).start()
        own(a, 3, B, left).wait_recv()
        fwd(a, 5, right, B, left).start()
        relay(a, 3, right, B).start()

    def late(a):
        own(a, 1, B, right).wait_recv()
        relay(a, 1, left, B).start()
        own(a, 2, A, left).wait_recv()
        relay(a, 2, right, A).start()

    def last(a):
        fwd(a, 4, far, A, right).wait_recv()
        relay(a, 4, far, A).start()
        fwd(a, 5, far, B, left).wait_recv()
        relay(a, 5, far, B).start()

    def norm(ch):
        @pl.loop(0, ROWS // 32)
        def _(r):
            rows = pl.ds(pl.multiple_of(r * 32, 32), 32)
            wide = T[ch, rows, :].astype(F32)
            inv = lax.rsqrt(jnp.mean(wide * wide, axis=1, keepdims=True) + EPS)
            N[ch, rows, :] = (wide * inv * gain[...]).astype(BF16)

    def chunk_cols(ch):
        return pl.ds(pl.multiple_of(ch * ROWS, ROWS), ROWS)

    def project(ch):
        cols = chunk_cols(ch)
        proj_t = jnp.dot(N[ch], WS[...], preferred_element_type=F32).T
        cos_, sin_ = cos[:, cols], sin[:, cols]
        q_t[0:64, cols] = rot_t(proj_t[0:64], cos_, sin_).astype(BF16)
        q_t[64:128, cols] = rot_t(proj_t[64:128], cos_, sin_).astype(BF16)
        both = jnp.concatenate([rot_t(proj_t[128:192], cos_, sin_), proj_t[192:256]], axis=0)
        kv_t[:, cols] = both.astype(BF16)
        kv[cols, :] = both.T.astype(BF16)

    def attend(ch):
        da_t[:, chunk_cols(ch)] = jnp.dot(
            G[ch], WO[...].reshape(D, 128), preferred_element_type=F32
        ).T.astype(BF16)

        @pl.loop(ch * 2, ch * 2 + 2)
        def _(i):
            attend_block(i)

    def attend_block(i):
        start = pl.multiple_of(jnp.maximum(i - 3, 0) * QB, QB)
        here = pl.ds(pl.multiple_of(i * QB, QB), QB)
        keys = kv[pl.ds(start, WIN), :]
        keys_t = kv_t[:, pl.ds(start, WIN)]
        q = (q_t[:, here].astype(F32) * (HEAD_DIM ** -0.5)).astype(BF16)
        da = da_t[:, here]
        none = jnp.zeros((64, 2 * QB), BF16)
        q2 = jnp.concatenate([q[0:64], q[64:128]], axis=1)
        da2 = jnp.concatenate([da[0:64], da[64:128]], axis=1)
        mixed = jnp.concatenate(
            [jnp.concatenate([q2, none], axis=1), jnp.concatenate([none, da2], axis=1)], axis=0
        )
        st = jnp.dot(keys, mixed, preferred_element_type=F32)
        key_pos = start + lax.broadcasted_iota(jnp.int32, (WIN, QB), 0)
        query_pos = i * QB + lax.broadcasted_iota(jnp.int32, (WIN, QB), 1)
        allowed = (key_pos >= begins[:, here]) & (key_pos <= query_pos)
        s = jnp.concatenate(
            [jnp.where(allowed, st[:, 0:QB], -1e30), jnp.where(allowed, st[:, QB : 2 * QB], -1e30)], axis=1
        )
        w = jnp.exp(s - jnp.max(s, axis=0, keepdims=True))
        p = w * (1.0 / jnp.sum(w, axis=0, keepdims=True))
        pb = p.astype(BF16)
        o = jnp.dot(keys_t, pb, preferred_element_type=F32)[64:128]
        delta = jnp.sum(da2.astype(F32) * o, axis=0, keepdims=True)
        ds = (p * (st[:, 2 * QB :] - delta)).astype(BF16)
        g = jnp.dot(keys_t, ds, preferred_element_type=F32)[0:64] * (HEAD_DIM ** -0.5)
        attn_t[0:64, here] = o[:, 0:QB].astype(BF16)
        attn_t[64:128, here] = o[:, QB:].astype(BF16)
        cos_, sin_ = cos[:, here], -sin[:, here]
        turned = jnp.concatenate([rot_t(g[:, 0:QB], cos_, sin_), rot_t(g[:, QB:], cos_, sin_)], axis=0)
        dq_t[:, here] = turned.astype(BF16)
        dq[here, :] = turned.T.astype(BF16)
        acc[pl.ds(start, WIN), :] += lax.dot_general(
            jnp.concatenate([ds, pb], axis=1), mixed, (((1,), (1,)), ((), ())), preferred_element_type=F32
        )

    acc[...] = jnp.zeros_like(acc)

    w_pass(0, 0)
    w_pass(1, 0)
    w_local.wait()
    for h in range(2):
        w_end(h, 0)
        w_start(h, 1)

    @pl.loop(1, ND)
    def _(k):
        gain_copy(k).wait()
        o_copy(k).start()

    for i in range(ND):
        gain[:, i * 128 : (i + 1) * 128] = GN[i, 0:1, :]
    norm(u)
    arrivals(0)
    start_own(1)
    own_relay(0).wait_recv()
    norm(mate)
    w_pass(0, 1)
    w_pass(1, 1)
    w_end(0, 1)
    w_end(1, 1)
    w_mate = remote(W.at[:, :, c], W.at[:, :, c], wps, wpr, mate, d)
    w_mate.start()
    late(0)

    @pl.loop(0, 2)
    def _(n):
        norm(((z + 1 + 2 * n) % 4) * 2 + c)

    last(0)
    for slot, rows in ((0, A), (1, B), (2, A), (3, B)):
        relay(0, slot, left, rows).wait_recv()

    @pl.loop(0, 3)
    def _(n):
        norm(jnp.where(n == 2, far, ((z + 1 + 2 * n) % 4) * 2 + (1 - c)))

    w_mate.wait()
    WS[:, 0:128] = W[:, :, :, :, pl.ds(pl.multiple_of(u * 128, 128), 128)].reshape(D, 128)
    k_tile = W[:, :, :, :, pl.ds(pl.multiple_of(QW + (z // 2) * 128, 128), 128)].reshape(D, 128)
    v_tile = W[:, :, :, :, pl.ds(pl.multiple_of(QW + KW + (z // 2) * 128, 128), 128)].reshape(D, 128)

    @pl.when(z % 2 == 0)
    def _():
        WS[:, 128:256] = jnp.concatenate([k_tile[:, 0:64], v_tile[:, 0:64]], axis=1)

    @pl.when(z % 2 == 1)
    def _():
        WS[:, 128:256] = jnp.concatenate([k_tile[:, 64:], v_tile[:, 64:]], axis=1)

    relay(0, 4, far, A).wait_recv()
    relay(0, 5, far, B).wait_recv()
    norm(((z + 2) % 4) * 2 + (1 - c))

    @pl.loop(0, NU)
    def _(n):
        project(n)

    @pl.loop(1, ND)
    def _(k):
        o_copy(k).wait()

    arrivals(1)
    own_relay(1).wait_recv()

    @pl.loop(0, 2)
    def _(n):
        attend(z * 2 + n)

    late(1)
    for slot, rows in ((0, A), (1, B), (2, A), (3, B)):
        relay(1, slot, left, rows).wait_recv()

    @pl.loop(0, 4)
    def _(n):
        attend(((z + 1 + 2 * (n // 2)) % 4) * 2 + n % 2)

    last(1)

    @pl.loop(0, 2)
    def _(n):
        @pl.when(n == 1)
        def _():
            relay(1, 4, far, A).wait_recv()
            relay(1, 5, far, B).wait_recv()

        attend(((z + 2) % 4) * 2 + (c + n) % 2)

    @pl.loop(0, NU)
    def _(b):
        cols = chunk_cols(b)
        t = acc[cols, :].T
        t = jnp.concatenate([rot_t(t[0:64], cos[:, cols], -sin[:, cols]), t[64:128]], axis=0)
        dkv[cols, :] = t.T.astype(BF16)

    def q_copy(k):
        to = (u + k) % NU
        rows = pl.ds(pl.multiple_of(to * ROWS, ROWS), ROWS)
        cols = pl.ds(pl.multiple_of(u * 128, 128), 128)
        return remote(dq.at[rows], DP.at[:, cols], qs.at[k], qr.at[k], to, d)

    def kv_copy(k):
        to = (u + k) % NU
        rows = pl.ds(pl.multiple_of(to * ROWS + c * 128, 128), 128)
        return remote(KVS.at[rows], RKV.at[z, pl.ds(pl.multiple_of(c * 128, 128), 128)], ks.at[k], kr.at[k], to, d)

    m_copy = remote(dkv, OT, ms, mr, mate, d)
    m_copy.start()

    @pl.loop(1, NU)
    def _(k):
        q_copy(k).start()

    DP[:, pl.ds(pl.multiple_of(u * 128, 128), 128)] = dq[pl.ds(pl.multiple_of(u * ROWS, ROWS), ROWS), :]

    def dw_block(f):
        cols = pl.ds(pl.multiple_of(f * 256, 256), 256)
        rows = pl.ds(pl.multiple_of(f * 16, 16), 16)
        q = jnp.dot(dq_t[...], N[:, :, cols].reshape(SEQ, 256), preferred_element_type=F32)
        R[:, :, rows, 0:128] = q.T.reshape(4, 4, 16, 128)
        o = jnp.dot(attn_t[...], G[:, :, cols].reshape(SEQ, 256), preferred_element_type=F32)
        R[:, :, rows, 128:256] = o.T.reshape(4, 4, 16, 128)

    dw_block(0)

    m_copy.wait()

    @pl.loop(0, NU)
    def _(b):
        rows = pl.ds(pl.multiple_of(b * ROWS, ROWS), ROWS)
        both = (dkv[rows, :].astype(F32) + OT[rows, :].astype(F32)).astype(BF16)
        KVS[rows, :] = both
        KVT[:, rows] = both.astype(F32).T.astype(BF16)

    @pl.loop(1, NU)
    def _(k):
        kv_copy(k).start()

    RKV[z, pl.ds(pl.multiple_of(c * 128, 128), 128), :] = KVS[
        pl.ds(pl.multiple_of(u * ROWS + c * 128, 128), 128), :
    ]

    @pl.loop(1, 5)
    def _(f):
        dw_block(f)

    def piece(h, st, step, part):
        rows = pl.ds(h * HALF + part * PART, PART)
        if along_x(h, st):
            j = (x + step) % 4
            return R.at[j, :, rows, :] if st == 0 else R.at[j, y, rows, :]
        j = (y + step) % 4
        return R.at[:, j, rows, :] if st == 0 else R.at[x, j, rows, :]

    def buf(h, st, slot):
        return B1.at[h, slot] if st == 0 else B2.at[h, slot]

    ROUTE = ((2, 0, 1), (2, 1, 3), (1, 1, 1), (3, 0, 3), (1, 0, 1), (3, 1, 3))

    def rcp(h, st, slot):
        step, part, to = ROUTE[slot]
        return remote(piece(h, st, step, part), buf(h, st, slot), rs.at[h, st, slot], rr.at[h, st, slot],
                      u, near(h, st, to))

    def start(h, st):
        for slot in range(4):
            rcp(h, st, slot).start()

    def pass_on(h, st):
        for slot, step, part in ((0, 1, 0), (1, 3, 1)):
            rcp(h, st, slot).wait_recv()
            p = piece(h, st, step, part)
            p[...] = p[...] + buf(h, st, slot)[...]
            rcp(h, st, slot + 4).start()

    def gather_up(h, st):
        for part, one, two in ((0, 3, 4), (1, 2, 5)):
            rcp(h, st, one).wait_recv()
            rcp(h, st, two).wait_recv()
            p = piece(h, st, 0, part)
            p[...] = p[...] + (buf(h, st, one)[...] + buf(h, st, two)[...])

    start(0, 0)

    @pl.loop(5, NU)
    def _(f):
        dw_block(f)

    for i in range(4):
        cols = pl.ds(pl.multiple_of((c * 4 + i) * 256, 256), 256)
        kvp = jnp.dot(KVT[...], N[:, :, cols].reshape(SEQ, 256), preferred_element_type=F32)
        R[:, :, 128 + (i // 2) * 16 : 144 + (i // 2) * 16, (i % 2) * 128 : (i % 2) * 128 + 128] = (
            kvp.T.reshape(4, 4, 16, 128)
        )

    start(1, 0)
    pass_on(0, 0)
    pass_on(1, 0)

    @pl.loop(1, NU)
    def _(k):
        q_copy(k).wait()
        kv_copy(k).wait()

    for i in range(2):
        a, b = RKV[2 * i], RKV[2 * i + 1]
        DP[:, QW + i * 128 : QW + (i + 1) * 128] = jnp.concatenate([a[:, 0:64], b[:, 0:64]], axis=1)
        DP[:, QW + KW + i * 128 : QW + KW + (i + 1) * 128] = jnp.concatenate([a[:, 64:], b[:, 64:]], axis=1)

    wide = tok[...].astype(F32)
    inv = lax.rsqrt(jnp.mean(wide * wide, axis=1, keepdims=True) + EPS)

    def back(f, along):
        cols = pl.ds(pl.multiple_of(f * 256, 256), 256)
        dn = lax.dot_general(DP[...], W[f // 2, pl.ds((f % 2) * 2, 2)].reshape(256, QW + 2 * KW), (((1,), (1,)), ((), ())), preferred_element_type=F32)
        unit = tok[:, cols].astype(F32) * inv
        gbuf[pl.ds(f, 1), :] = jnp.sum(dn * unit, axis=0, keepdims=True)
        scaled = dn * gain[:, cols]
        DN[f] = scaled
        return along + jnp.sum(scaled * unit, axis=1, keepdims=True)

    along = lax.fori_loop(0, NU, back, jnp.zeros((ROWS, 1), F32))
    mean = along * (1.0 / D)

    def g_copy(k):
        return remote(gbuf, GR.at[d], gs.at[k], gr.at[k], u, (d + k) % ND)

    @pl.loop(1, ND)
    def _(k):
        g_copy(k).start()

    GR[d] = gbuf[...]

    gather_up(0, 0)
    start(0, 1)
    gather_up(1, 0)
    start(1, 1)

    @pl.loop(0, NU)
    def _(f):
        cols = pl.ds(pl.multiple_of(f * 256, 256), 256)
        unit = tok[:, cols].astype(F32) * inv
        d_rows = inv * (DN[f] - unit * mean)
        dtok_o[:, cols] = (dout[:, cols].astype(F32) + d_rows).astype(BF16)

    pass_on(0, 1)
    pass_on(1, 1)

    @pl.loop(1, ND)
    def _(k):
        g_copy(k).wait()

    gsum[...] = jnp.sum(GR[...], axis=0)

    def gu_copy(k):
        return remote(gsum, GU.at[u], us.at[k], ur.at[k], (u + k) % NU, d)

    @pl.loop(1, NU)
    def _(k):
        gu_copy(k).start()

    GU[u] = gsum[...]
    gather_up(0, 1)
    gather_up(1, 1)

    def f_copy(k):
        to = (u + k) % NU
        return remote(R.at[x, y, pl.ds(pl.multiple_of(to * 16, 16), 16)], FIN.at[u], fs.at[k], fr.at[k], to, d)

    @pl.loop(1, NU)
    def _(k):
        f_copy(k).start()

    def v_block(i):
        return R.at[x, y, pl.ds(128 + (i // 2) * 16, 16), pl.ds((i % 2) * 128, 128)]

    def v_copy(i):
        return remote(v_block(i), FKV.at[z], vs.at[i], vr.at[z], c * 4 + i, d)

    def v_arrival(zs):
        return remote(v_block(0), FKV.at[zs], vs.at[0], vr.at[zs], u, d)

    for i in range(4):
        @pl.when(c * 4 + i != u)
        def _():
            v_copy(i).start()

        @pl.when(c * 4 + i == u)
        def _():
            FKV[z] = v_block(i)[...]

    FIN[u] = R[x, y, pl.ds(pl.multiple_of(u * 16, 16), 16), :]

    @pl.loop(1, NU)
    def _(k):
        gu_copy(k).wait()

    ggain_o[...] = jnp.sum(GU[...], axis=0) * FACTOR

    @pl.loop(1, NU)
    def _(k):
        f_copy(k).wait()

    for i in range(4):
        @pl.when(i * 2 + u // 4 != u)
        def _():
            v_arrival(i).wait_recv()

        @pl.when(c * 4 + i != u)
        def _():
            v_copy(i).wait_send()

    for i in range(NU):
        gqkv_o[:, i * 128 : (i + 1) * 128] = FIN[i, :, 0:128] * FACTOR
        gout_o[:, i * 128 : (i + 1) * 128] = FIN[i, :, 128:256] * FACTOR
    for i in range(2):
        a, b = FKV[2 * i] * FACTOR, FKV[2 * i + 1] * FACTOR
        gqkv_o[:, QW + i * 128 : QW + (i + 1) * 128] = jnp.concatenate([a[:, 0:64], b[:, 0:64]], axis=1)
        gqkv_o[:, QW + KW + i * 128 : QW + KW + (i + 1) * 128] = jnp.concatenate([a[:, 64:], b[:, 64:]], axis=1)

    for h in range(2):
        for st in range(2):
            for slot in range(6):
                rcp(h, st, slot).wait_send()


    for h in range(2):
        for st in range(2):
            for slot in range(6):
                w_copy(h, st, slot).wait_send()
    for a in range(2):
        own(a, 0, A, right).wait_send()
        own(a, 1, B, right).wait_send()
        own(a, 2, A, left).wait_send()
        own(a, 3, B, left).wait_send()
        fwd(a, 4, left, A, right).wait_send()
        fwd(a, 5, right, B, left).wait_send()
        own_relay(a).wait_send()
        relay(a, 0, left, A).wait_send()
        relay(a, 1, left, B).wait_send()
        relay(a, 2, right, A).wait_send()
        relay(a, 3, right, B).wait_send()
        relay(a, 4, far, A).wait_send()
        relay(a, 5, far, B).wait_send()


def block_step(tok, dout, begins, cos, sin, gain, wqkv, wout):
    dma = pltpu.SemaphoreType.DMA
    vmem = pl.BlockSpec(memory_space=pltpu.VMEM)
    V = pltpu.VMEM
    return pl.pallas_call(
        step_kernel,
        name="block_step",
        out_shape=(
            jax.ShapeDtypeStruct((ROWS, D), BF16),
            jax.ShapeDtypeStruct((16, QW + 2 * KW), F32),
            jax.ShapeDtypeStruct((16, QW), F32),
            jax.ShapeDtypeStruct((NU, 256), F32),
        ),
        in_specs=[vmem] * 8,
        out_specs=(vmem,) * 4,
        scratch_shapes=[
            V((NU, ROWS, D), BF16), V((NU, ROWS, D), BF16), V((NU, ROWS, D), BF16),
            V((4, 4, 2, 64, QW + 2 * KW), BF16), V((ND, 128, 128), BF16), V((ND, 8, 128), F32),
            V((8, 128), F32), V((1, D), F32), V((D, 256), BF16),
            V((128, SEQ), BF16), V((128, SEQ), BF16), V((SEQ, 128), BF16), V((128, SEQ), BF16),
            V((128, SEQ), BF16), V((128, SEQ), BF16), V((SEQ, 128), BF16), V((SEQ, 128), BF16),
            V((SEQ, 128), F32),
            V((ROWS, QW + 2 * KW), BF16), V((4, ROWS, 128), BF16),
            V((SEQ, 128), BF16), V((SEQ, 128), BF16), V((128, SEQ), BF16),
            V((4, 4, 2 * HALF, 256), F32), V((2, 6, 4, PART, 256), F32), V((2, 6, PART, 256), F32),
            V((NU, 16, 256), F32), V((4, 16, 128), F32), V((NU, ROWS, 256), F32),
            V((NU, 256), F32), V((ND, NU, 256), F32), V((NU, 256), F32), V((NU, NU, 256), F32),
            dma((2, 6)), dma((2, 6)), dma((2, 7)), dma((2, 7)), dma((2, 2, 6)), dma((2, 2, 6)),
            dma((ND,)), dma((ND,)), dma((ND,)), dma((ND,)), dma, dma, dma,
            dma, dma, dma((NU,)), dma((NU,)), dma((NU,)), dma((NU,)),
            dma((2, 2, 6)), dma((2, 2, 6)), dma((NU,)), dma((NU,)), dma((4,)), dma((4,)),
            dma((ND,)), dma((ND,)), dma((NU,)), dma((NU,)),
        ],
        compiler_params=pltpu.CompilerParams(
            collective_id=0, has_side_effects=True, vmem_limit_bytes=62 * 1024 * 1024
        ),
    )(tok, dout, begins, cos, sin, gain, wqkv, wout)


def body(tokens, d_out, lengths, gain, w_qkv, w_out):
    u = lax.axis_index("ulysses")
    d = lax.axis_index("dp")
    begins, places = doc_positions(lengths[0], SEQ)
    cos_t, sin_t = rotary_tables_t(places)
    d_tokens, grad_qkv, grad_out, gain_sum = block_step(
        tokens[0], d_out[0], begins[None, :], cos_t, sin_t, gain[None, :], w_qkv, w_out
    )
    grad_gain = lax.dynamic_slice(gain_sum, (u, d * 16), (1, 16)).reshape(16)
    return d_tokens[None], grad_qkv, grad_out, grad_gain


def solution(mesh):
    in_specs = (
        P("dp", "ulysses", None),
        P("dp", "ulysses", None),
        P("dp", None),
        P("dp"),
        P("dp", None),
        P("dp", None),
    )
    out_specs = (
        P("dp", "ulysses", None),
        P(("ulysses", "dp"), None),
        P(("ulysses", "dp"), None),
        P(("ulysses", "dp")),
    )
    return jax.shard_map(body, mesh=mesh, in_specs=in_specs, out_specs=out_specs, check_vma=False)
```

```python
import math

import jax
import jax.numpy as jnp
from jax import lax
from jax.experimental import pallas as pl
from jax.experimental.pallas import tpu as pltpu
from jax.sharding import PartitionSpec as P

HEADS = 16
KV_HEADS = 4
HEAD_DIM = 64
D = 2048
SEQ = 2048
ROWS = 256
QW = 1024
KW = 256
NU = 8
ND = 16
EPS = 1e-05
ROPE_BASE = 500000.0
MESH = pl.DeviceIdType.MESH
F32 = jnp.float32
BF16 = jnp.bfloat16


def doc_positions(doc_lengths, length):
    order = jnp.arange(doc_lengths.shape[0])
    bounds = jnp.sum(jnp.where(order[None, :] < order[:, None], doc_lengths[None, :], 0), axis=1)
    places = jnp.arange(length, dtype=jnp.int32)
    begins = jnp.max(jnp.where(bounds[None, :] <= places[:, None], bounds[None, :], 0), axis=1)
    return begins, places - begins


def rotary_tables_t(places):
    inverse = ROPE_BASE ** (-jnp.arange(0, HEAD_DIM, 2).astype(F32) / HEAD_DIM)
    angles = inverse[:, None] * places.astype(F32)[None, :]
    return jnp.cos(angles), jnp.sin(angles)


def remote(src, dst, send_sem, recv_sem, u, d):
    return pltpu.make_async_remote_copy(
        src_ref=src, dst_ref=dst, send_sem=send_sem, recv_sem=recv_sem,
        device_id={"ulysses": u, "dp": d}, device_id_type=MESH,
    )


QB = 128
WIN = 512
FACTOR = 1.0 / math.sqrt(SEQ * ND)
HALF = 80
PART = 40


def rot_t(u, cos, sin):
    a, b = u[: HEAD_DIM // 2], u[HEAD_DIM // 2 :]
    return jnp.concatenate([a * cos - b * sin, b * cos + a * sin], axis=0)


def step_kernel(tok, dout, begins, cos, sin, gain_in, wqkv, wout,
                dtok_o, gqkv_o, gout_o, ggain_o,
                T, N, G, W, WO, GN, gain_rows, gain, WS, q_t, kv_t, kv, da_t, attn_t, dq_t, dq, dkv, acc,
                DP, RKV, OT, KVS, KVT, R, B1, B2, FIN, FKV, DN, gbuf, GR, gsum, GU,
                zs, zr, ps, pr, ws, wr, os_, or_, gns, gnr, wps, wpr, loc,
                ms, mr, qs, qr, ks, kr, rs, rr, fs, fr, vs, vr, gs, gr, us, ur):
    u = lax.axis_index("ulysses")
    d = lax.axis_index("dp")
    z, c = u // 2, u % 2
    x, y = d // 4, d % 4
    right = ((z + 1) % 4) * 2 + c
    left = ((z + 3) % 4) * 2 + c
    far = ((z + 2) % 4) * 2 + c
    mate = z * 2 + (1 - c)

    gain_rows[...] = jnp.broadcast_to(gain_in[...].astype(F32), (8, 128))
    barrier = pltpu.get_barrier_semaphore()

    @pl.loop(1, NU)
    def _(k):
        pl.semaphore_signal(barrier, inc=1, device_id={"ulysses": (u + k) % NU, "dp": d}, device_id_type=MESH)

    @pl.loop(1, ND)
    def _(k):
        pl.semaphore_signal(barrier, inc=1, device_id={"ulysses": u, "dp": (d + k) % ND}, device_id_type=MESH)

    pl.semaphore_wait(barrier, NU + ND - 2)

    H = ROWS // 2
    A, B = pl.ds(0, H), pl.ds(H, H)
    srcs, dsts = (tok, dout), (T, G)

    def own(a, slot, rows, to):
        return remote(srcs[a].at[rows], dsts[a].at[u, rows], zs.at[a, slot], zr.at[a, slot], to, d)

    def fwd(a, slot, frm, rows, to):
        return remote(dsts[a].at[frm, rows], dsts[a].at[frm, rows], zs.at[a, slot], zr.at[a, slot], to, d)

    def relay(a, slot, frm, rows):
        return remote(dsts[a].at[frm, rows], dsts[a].at[frm, rows], ps.at[a, slot], pr.at[a, slot], mate, d)

    def own_relay(a):
        return remote(srcs[a], dsts[a].at[u], ps.at[a, 6], pr.at[a, 6], mate, d)

    def start_own(a):
        own(a, 0, A, right).start()
        own(a, 3, B, left).start()
        own(a, 1, B, right).start()
        own(a, 2, A, left).start()
        own_relay(a).start()

    start_own(0)

    def along_x(h, st):
        return (h == 0) == (st == 0)

    def near(h, st, step):
        if along_x(h, st):
            return ((x + step) % 4) * 4 + y
        return x * 4 + (y + step) % 4

    def w_piece(h, st, step, part):
        rows = pl.ds(h * 32 + part * 16, 16)
        if along_x(h, st):
            j = (x + step) % 4
            return W.at[j, y, c, rows] if st == 0 else W.at[j, :, c, rows]
        j = (y + step) % 4
        return W.at[x, j, c, rows] if st == 0 else W.at[:, j, c, rows]

    W_ROUTE = ((0, 0, 1), (0, 1, 3), (0, 1, 1), (0, 0, 3), (3, 0, 1), (1, 1, 3))

    def w_copy(h, st, slot):
        step, part, to = W_ROUTE[slot]
        if st == 0 and step == 0:
            src = wqkv.at[pl.ds(c * 64 + h * 32 + part * 16, 16)]
        else:
            src = w_piece(h, st, step, part)
        return remote(src, w_piece(h, st, step, part), ws.at[h, st, slot], wr.at[h, st, slot], u, near(h, st, to))

    def w_start(h, st):
        for slot in range(4):
            w_copy(h, st, slot).start()

    def w_pass(h, st):
        for slot in range(2):
            w_copy(h, st, slot).wait_recv()
            w_copy(h, st, slot + 4).start()

    def w_end(h, st):
        for slot in range(2, 6):
            w_copy(h, st, slot).wait_recv()

    def o_copy(k):
        to = (d + k) % ND
        return remote(wout.at[:, pl.ds(pl.multiple_of(u * 128, 128), 128)], WO.at[d], os_.at[k], or_.at[k], u, to)

    def gain_copy(k):
        to = (d + k) % ND
        return remote(gain_rows, GN.at[d], gns.at[k], gnr.at[k], u, to)

    w_local = pltpu.make_async_copy(wqkv.at[pl.ds(c * 64, 64)], W.at[x, y, c], loc)
    w_local.start()
    w_start(0, 0)
    w_start(1, 0)

    @pl.loop(1, ND)
    def _(k):
        gain_copy(k).start()

    T[u] = tok[...]
    G[u] = dout[...]
    GN[d] = gain_rows[...]
    WO[d] = wout[:, pl.ds(pl.multiple_of(u * 128, 128), 128)]

    def arrivals(a):
        own(a, 0, A, right).wait_recv()
        fwd(a, 4, left, A, right).start()
        relay(a, 0, left, A).start()
        own(a, 3, B, left).wait_recv()
        fwd(a, 5, right, B, left).start()
        relay(a, 3, right, B).start()

    def late(a):
        own(a, 1, B, right).wait_recv()
        relay(a, 1, left, B).start()
        own(a, 2, A, left).wait_recv()
        relay(a, 2, right, A).start()

    def last(a):
        fwd(a, 4, far, A, right).wait_recv()
        relay(a, 4, far, A).start()
        fwd(a, 5, far, B, left).wait_recv()
        relay(a, 5, far, B).start()

    def norm(ch):
        @pl.loop(0, ROWS // 32)
        def _(r):
            rows = pl.ds(pl.multiple_of(r * 32, 32), 32)
            wide = T[ch, rows, :].astype(F32)
            inv = lax.rsqrt(jnp.mean(wide * wide, axis=1, keepdims=True) + EPS)
            N[ch, rows, :] = (wide * inv * gain[...]).astype(BF16)

    def chunk_cols(ch):
        return pl.ds(pl.multiple_of(ch * ROWS, ROWS), ROWS)

    def project(ch):
        cols = chunk_cols(ch)
        proj_t = jnp.dot(N[ch], WS[...], preferred_element_type=F32).T
        cos_, sin_ = cos[:, cols], sin[:, cols]
        q_t[0:64, cols] = rot_t(proj_t[0:64], cos_, sin_).astype(BF16)
        q_t[64:128, cols] = rot_t(proj_t[64:128], cos_, sin_).astype(BF16)
        both = jnp.concatenate([rot_t(proj_t[128:192], cos_, sin_), proj_t[192:256]], axis=0)
        kv_t[:, cols] = both.astype(BF16)
        kv[cols, :] = both.T.astype(BF16)

    def attend(*blocks):
        for i in blocks:
            da_t[:, pl.ds(pl.multiple_of(i * QB, QB), QB)] = jnp.dot(
                G[i // 2, pl.ds(pl.multiple_of((i % 2) * QB, QB), QB), :], WO[...].reshape(D, 128),
                preferred_element_type=F32,
            ).T.astype(BF16)
        for i in blocks:
            attend_block(i)

    def attend_block(i):
        start = pl.multiple_of(jnp.maximum(i - 3, 0) * QB, QB)
        here = pl.ds(pl.multiple_of(i * QB, QB), QB)
        keys = kv[pl.ds(start, WIN), :]
        keys_t = kv_t[:, pl.ds(start, WIN)]
        q = (q_t[:, here].astype(F32) * (HEAD_DIM ** -0.5)).astype(BF16)
        da = da_t[:, here]
        none = jnp.zeros((64, 2 * QB), BF16)
        q2 = jnp.concatenate([q[0:64], q[64:128]], axis=1)
        da2 = jnp.concatenate([da[0:64], da[64:128]], axis=1)
        mixed = jnp.concatenate(
            [jnp.concatenate([q2, none], axis=1), jnp.concatenate([none, da2], axis=1)], axis=0
        )
        st = jnp.dot(keys, mixed, preferred_element_type=F32)
        key_pos = start + lax.broadcasted_iota(jnp.int32, (WIN, QB), 0)
        query_pos = i * QB + lax.broadcasted_iota(jnp.int32, (WIN, QB), 1)
        allowed = (key_pos >= begins[:, here]) & (key_pos <= query_pos)
        s = jnp.concatenate(
            [jnp.where(allowed, st[:, 0:QB], -1e30), jnp.where(allowed, st[:, QB : 2 * QB], -1e30)], axis=1
        )
        w = jnp.exp(s - jnp.max(s, axis=0, keepdims=True))
        p = w * (1.0 / jnp.sum(w, axis=0, keepdims=True))
        pb = p.astype(BF16)
        o = jnp.dot(keys_t, pb, preferred_element_type=F32)[64:128]
        delta = jnp.sum(da2.astype(F32) * o, axis=0, keepdims=True)
        ds = (p * (st[:, 2 * QB :] - delta)).astype(BF16)
        g = jnp.dot(keys_t, ds, preferred_element_type=F32)[0:64] * (HEAD_DIM ** -0.5)
        attn_t[0:64, here] = o[:, 0:QB].astype(BF16)
        attn_t[64:128, here] = o[:, QB:].astype(BF16)
        cos_, sin_ = cos[:, here], -sin[:, here]
        turned = jnp.concatenate([rot_t(g[:, 0:QB], cos_, sin_), rot_t(g[:, QB:], cos_, sin_)], axis=0)
        dq_t[:, here] = turned.astype(BF16)
        dq[here, :] = turned.T.astype(BF16)
        acc[pl.ds(start, WIN), :] += lax.dot_general(
            jnp.concatenate([ds, pb], axis=1), mixed, (((1,), (1,)), ((), ())), preferred_element_type=F32
        )

    acc[...] = jnp.zeros_like(acc)

    w_pass(0, 0)
    w_pass(1, 0)
    w_local.wait()
    for h in range(2):
        w_end(h, 0)
        w_start(h, 1)

    @pl.loop(1, ND)
    def _(k):
        gain_copy(k).wait()
        o_copy(k).start()

    for i in range(ND):
        gain[:, i * 128 : (i + 1) * 128] = GN[i, 0:1, :]
    norm(u)
    arrivals(0)
    start_own(1)
    own_relay(0).wait_recv()
    norm(mate)
    w_pass(0, 1)
    w_pass(1, 1)
    w_end(0, 1)
    w_end(1, 1)
    w_mate = remote(W.at[:, :, c], W.at[:, :, c], wps, wpr, mate, d)
    w_mate.start()
    late(0)

    @pl.loop(0, 2)
    def _(n):
        norm(((z + 1 + 2 * n) % 4) * 2 + c)

    last(0)
    for slot, rows in ((0, A), (1, B), (2, A), (3, B)):
        relay(0, slot, left, rows).wait_recv()

    @pl.loop(0, 3)
    def _(n):
        norm(jnp.where(n == 2, far, ((z + 1 + 2 * n) % 4) * 2 + (1 - c)))

    w_mate.wait()
    WS[:, 0:128] = W[:, :, :, :, pl.ds(pl.multiple_of(u * 128, 128), 128)].reshape(D, 128)
    k_tile = W[:, :, :, :, pl.ds(pl.multiple_of(QW + (z // 2) * 128, 128), 128)].reshape(D, 128)
    v_tile = W[:, :, :, :, pl.ds(pl.multiple_of(QW + KW + (z // 2) * 128, 128), 128)].reshape(D, 128)

    @pl.when(z % 2 == 0)
    def _():
        WS[:, 128:256] = jnp.concatenate([k_tile[:, 0:64], v_tile[:, 0:64]], axis=1)

    @pl.when(z % 2 == 1)
    def _():
        WS[:, 128:256] = jnp.concatenate([k_tile[:, 64:], v_tile[:, 64:]], axis=1)

    relay(0, 4, far, A).wait_recv()
    relay(0, 5, far, B).wait_recv()
    norm(((z + 2) % 4) * 2 + (1 - c))

    @pl.loop(0, NU)
    def _(n):
        project(n)

    @pl.loop(1, ND)
    def _(k):
        o_copy(k).wait()

    arrivals(1)
    own_relay(1).wait_recv()

    @pl.loop(0, 2)
    def _(n):
        attend((z * 2 + n) * 2, (z * 2 + n) * 2 + 1)

    def attend_near(first):
        @pl.loop(0, 2)
        def _(n):
            base = ((z + 3 + 2 * n) % 4) * 4
            half = n if first else 1 - n
            attend(base + half, base + 2 + half)

    relay(1, 0, left, A).wait_recv()
    relay(1, 3, left, B).wait_recv()
    attend_near(True)
    late(1)
    relay(1, 1, left, B).wait_recv()
    relay(1, 2, left, A).wait_recv()
    attend_near(False)

    def dw(f, steps, add):
        cols = pl.ds(pl.multiple_of(f * 256, 256), 256)
        q = o = 0.0
        for step in steps:
            zz = (z + step) % 4
            toks = pl.ds(pl.multiple_of(zz * 512, 512), 512)
            q += jnp.dot(dq_t[:, toks], N[pl.ds(zz * 2, 2), :, cols].reshape(512, 256), preferred_element_type=F32)
            o += jnp.dot(attn_t[:, toks], G[pl.ds(zz * 2, 2), :, cols].reshape(512, 256), preferred_element_type=F32)
        rows = pl.ds(pl.multiple_of(f * 16, 16), 16)
        both = jnp.concatenate([q.T, o.T], axis=1).reshape(4, 4, 16, 256)
        R[:, :, rows, :] = R[:, :, rows, :] + both if add else both

    @pl.loop(0, NU)
    def _(f):
        dw(f, (0, 1, 3), False)

    last(1)

    @pl.loop(0, 2)
    def _(n):
        @pl.when(n == 1)
        def _():
            relay(1, 4, far, A).wait_recv()
            relay(1, 5, far, B).wait_recv()

        ch = ((z + 2) % 4) * 2 + (c + n) % 2
        attend(ch * 2, ch * 2 + 1)

    @pl.loop(0, NU)
    def _(b):
        cols = chunk_cols(b)
        t = acc[cols, :].T
        t = jnp.concatenate([rot_t(t[0:64], cos[:, cols], -sin[:, cols]), t[64:128]], axis=0)
        dkv[cols, :] = t.T.astype(BF16)

    def q_copy(k):
        to = (u + k) % NU
        rows = pl.ds(pl.multiple_of(to * ROWS, ROWS), ROWS)
        cols = pl.ds(pl.multiple_of(u * 128, 128), 128)
        return remote(dq.at[rows], DP.at[:, cols], qs.at[k], qr.at[k], to, d)

    def kv_copy(k):
        to = (u + k) % NU
        rows = pl.ds(pl.multiple_of(to * ROWS + c * 128, 128), 128)
        return remote(KVS.at[rows], RKV.at[z, pl.ds(pl.multiple_of(c * 128, 128), 128)], ks.at[k], kr.at[k], to, d)

    m_copy = remote(dkv, OT, ms, mr, mate, d)
    m_copy.start()

    @pl.loop(1, NU)
    def _(k):
        q_copy(k).start()

    DP[:, pl.ds(pl.multiple_of(u * 128, 128), 128)] = dq[pl.ds(pl.multiple_of(u * ROWS, ROWS), ROWS), :]

    def piece(h, st, step, part):
        rows = pl.ds(h * HALF + part * PART, PART)
        if along_x(h, st):
            j = (x + step) % 4
            return R.at[j, :, rows, :] if st == 0 else R.at[j, y, rows, :]
        j = (y + step) % 4
        return R.at[:, j, rows, :] if st == 0 else R.at[x, j, rows, :]

    def buf(h, st, slot):
        return B1.at[h, slot] if st == 0 else B2.at[h, slot]

    ROUTE = ((2, 0, 1), (2, 1, 3), (1, 1, 1), (3, 0, 3), (1, 0, 1), (3, 1, 3))

    def rcp(h, st, slot):
        step, part, to = ROUTE[slot]
        return remote(piece(h, st, step, part), buf(h, st, slot), rs.at[h, st, slot], rr.at[h, st, slot],
                      u, near(h, st, to))

    def start(h, st):
        for slot in range(4):
            rcp(h, st, slot).start()

    def pass_on(h, st):
        for slot, step, part in ((0, 1, 0), (1, 3, 1)):
            rcp(h, st, slot).wait_recv()
            p = piece(h, st, step, part)
            p[...] = p[...] + buf(h, st, slot)[...]
            rcp(h, st, slot + 4).start()

    def gather_up(h, st):
        for part, one, two in ((0, 3, 4), (1, 2, 5)):
            rcp(h, st, one).wait_recv()
            rcp(h, st, two).wait_recv()
            p = piece(h, st, 0, part)
            p[...] = p[...] + (buf(h, st, one)[...] + buf(h, st, two)[...])

    @pl.loop(0, 5)
    def _(f):
        dw(f, (2,), True)

    start(0, 0)

    @pl.loop(5, NU)
    def _(f):
        dw(f, (2,), True)

    m_copy.wait()

    @pl.loop(0, NU)
    def _(b):
        rows = pl.ds(pl.multiple_of(b * ROWS, ROWS), ROWS)
        both = (dkv[rows, :].astype(F32) + OT[rows, :].astype(F32)).astype(BF16)
        KVS[rows, :] = both
        KVT[:, rows] = both.astype(F32).T.astype(BF16)

    @pl.loop(1, NU)
    def _(k):
        kv_copy(k).start()

    RKV[z, pl.ds(pl.multiple_of(c * 128, 128), 128), :] = KVS[
        pl.ds(pl.multiple_of(u * ROWS + c * 128, 128), 128), :
    ]

    for i in range(4):
        cols = pl.ds(pl.multiple_of((c * 4 + i) * 256, 256), 256)
        kvp = jnp.dot(KVT[...], N[:, :, cols].reshape(SEQ, 256), preferred_element_type=F32)
        R[:, :, 128 + (i // 2) * 16 : 144 + (i // 2) * 16, (i % 2) * 128 : (i % 2) * 128 + 128] = (
            kvp.T.reshape(4, 4, 16, 128)
        )

    start(1, 0)
    pass_on(0, 0)
    pass_on(1, 0)

    @pl.loop(1, NU)
    def _(k):
        q_copy(k).wait()
        kv_copy(k).wait()

    for i in range(2):
        a, b = RKV[2 * i], RKV[2 * i + 1]
        DP[:, QW + i * 128 : QW + (i + 1) * 128] = jnp.concatenate([a[:, 0:64], b[:, 0:64]], axis=1)
        DP[:, QW + KW + i * 128 : QW + KW + (i + 1) * 128] = jnp.concatenate([a[:, 64:], b[:, 64:]], axis=1)

    wide = tok[...].astype(F32)
    inv = lax.rsqrt(jnp.mean(wide * wide, axis=1, keepdims=True) + EPS)

    def back(f, along):
        cols = pl.ds(pl.multiple_of(f * 256, 256), 256)
        dn = lax.dot_general(DP[...], W[f // 2, pl.ds((f % 2) * 2, 2)].reshape(256, QW + 2 * KW), (((1,), (1,)), ((), ())), preferred_element_type=F32)
        unit = tok[:, cols].astype(F32) * inv
        gbuf[pl.ds(f, 1), :] = jnp.sum(dn * unit, axis=0, keepdims=True)
        scaled = dn * gain[:, cols]
        DN[f] = scaled
        return along + jnp.sum(scaled * unit, axis=1, keepdims=True)

    along = lax.fori_loop(0, NU, back, jnp.zeros((ROWS, 1), F32))
    mean = along * (1.0 / D)

    def g_copy(k):
        return remote(gbuf, GR.at[d], gs.at[k], gr.at[k], u, (d + k) % ND)

    @pl.loop(1, ND)
    def _(k):
        g_copy(k).start()

    GR[d] = gbuf[...]

    gather_up(0, 0)
    start(0, 1)
    gather_up(1, 0)
    start(1, 1)

    @pl.loop(0, NU)
    def _(f):
        cols = pl.ds(pl.multiple_of(f * 256, 256), 256)
        unit = tok[:, cols].astype(F32) * inv
        d_rows = inv * (DN[f] - unit * mean)
        dtok_o[:, cols] = (dout[:, cols].astype(F32) + d_rows).astype(BF16)

    pass_on(0, 1)
    pass_on(1, 1)

    @pl.loop(1, ND)
    def _(k):
        g_copy(k).wait()

    gsum[...] = jnp.sum(GR[...], axis=0)

    def gu_copy(k):
        return remote(gsum, GU.at[u], us.at[k], ur.at[k], (u + k) % NU, d)

    @pl.loop(1, NU)
    def _(k):
        gu_copy(k).start()

    GU[u] = gsum[...]
    gather_up(0, 1)
    gather_up(1, 1)

    def f_copy(k):
        to = (u + k) % NU
        return remote(R.at[x, y, pl.ds(pl.multiple_of(to * 16, 16), 16)], FIN.at[u], fs.at[k], fr.at[k], to, d)

    @pl.loop(1, NU)
    def _(k):
        f_copy(k).start()

    def v_block(i):
        return R.at[x, y, pl.ds(128 + (i // 2) * 16, 16), pl.ds((i % 2) * 128, 128)]

    def v_copy(i):
        return remote(v_block(i), FKV.at[z], vs.at[i], vr.at[z], c * 4 + i, d)

    def v_arrival(zs):
        return remote(v_block(0), FKV.at[zs], vs.at[0], vr.at[zs], u, d)

    for i in range(4):
        @pl.when(c * 4 + i != u)
        def _():
            v_copy(i).start()

        @pl.when(c * 4 + i == u)
        def _():
            FKV[z] = v_block(i)[...]

    FIN[u] = R[x, y, pl.ds(pl.multiple_of(u * 16, 16), 16), :]

    @pl.loop(1, NU)
    def _(k):
        gu_copy(k).wait()

    ggain_o[...] = jnp.sum(GU[...], axis=0) * FACTOR

    @pl.loop(1, NU)
    def _(k):
        f_copy(k).wait()

    for i in range(4):
        @pl.when(i * 2 + u // 4 != u)
        def _():
            v_arrival(i).wait_recv()

        @pl.when(c * 4 + i != u)
        def _():
            v_copy(i).wait_send()

    for i in range(NU):
        gqkv_o[:, i * 128 : (i + 1) * 128] = FIN[i, :, 0:128] * FACTOR
        gout_o[:, i * 128 : (i + 1) * 128] = FIN[i, :, 128:256] * FACTOR
    for i in range(2):
        a, b = FKV[2 * i] * FACTOR, FKV[2 * i + 1] * FACTOR
        gqkv_o[:, QW + i * 128 : QW + (i + 1) * 128] = jnp.concatenate([a[:, 0:64], b[:, 0:64]], axis=1)
        gqkv_o[:, QW + KW + i * 128 : QW + KW + (i + 1) * 128] = jnp.concatenate([a[:, 64:], b[:, 64:]], axis=1)

    for h in range(2):
        for st in range(2):
            for slot in range(6):
                rcp(h, st, slot).wait_send()


    for h in range(2):
        for st in range(2):
            for slot in range(6):
                w_copy(h, st, slot).wait_send()
    for a in range(2):
        own(a, 0, A, right).wait_send()
        own(a, 1, B, right).wait_send()
        own(a, 2, A, left).wait_send()
        own(a, 3, B, left).wait_send()
        fwd(a, 4, left, A, right).wait_send()
        fwd(a, 5, right, B, left).wait_send()
        own_relay(a).wait_send()
        relay(a, 0, left, A).wait_send()
        relay(a, 1, left, B).wait_send()
        relay(a, 2, right, A).wait_send()
        relay(a, 3, right, B).wait_send()
        relay(a, 4, far, A).wait_send()
        relay(a, 5, far, B).wait_send()


def block_step(tok, dout, begins, cos, sin, gain, wqkv, wout):
    dma = pltpu.SemaphoreType.DMA
    vmem = pl.BlockSpec(memory_space=pltpu.VMEM)
    V = pltpu.VMEM
    return pl.pallas_call(
        step_kernel,
        name="block_step",
        out_shape=(
            jax.ShapeDtypeStruct((ROWS, D), BF16),
            jax.ShapeDtypeStruct((16, QW + 2 * KW), F32),
            jax.ShapeDtypeStruct((16, QW), F32),
            jax.ShapeDtypeStruct((NU, 256), F32),
        ),
        in_specs=[vmem] * 8,
        out_specs=(vmem,) * 4,
        scratch_shapes=[
            V((NU, ROWS, D), BF16), V((NU, ROWS, D), BF16), V((NU, ROWS, D), BF16),
            V((4, 4, 2, 64, QW + 2 * KW), BF16), V((ND, 128, 128), BF16), V((ND, 8, 128), F32),
            V((8, 128), F32), V((1, D), F32), V((D, 256), BF16),
            V((128, SEQ), BF16), V((128, SEQ), BF16), V((SEQ, 128), BF16), V((128, SEQ), BF16),
            V((128, SEQ), BF16), V((128, SEQ), BF16), V((SEQ, 128), BF16), V((SEQ, 128), BF16),
            V((SEQ, 128), F32),
            V((ROWS, QW + 2 * KW), BF16), V((4, ROWS, 128), BF16),
            V((SEQ, 128), BF16), V((SEQ, 128), BF16), V((128, SEQ), BF16),
            V((4, 4, 2 * HALF, 256), F32), V((2, 6, 4, PART, 256), F32), V((2, 6, PART, 256), F32),
            V((NU, 16, 256), F32), V((4, 16, 128), F32), V((NU, ROWS, 256), F32),
            V((NU, 256), F32), V((ND, NU, 256), F32), V((NU, 256), F32), V((NU, NU, 256), F32),
            dma((2, 6)), dma((2, 6)), dma((2, 7)), dma((2, 7)), dma((2, 2, 6)), dma((2, 2, 6)),
            dma((ND,)), dma((ND,)), dma((ND,)), dma((ND,)), dma, dma, dma,
            dma, dma, dma((NU,)), dma((NU,)), dma((NU,)), dma((NU,)),
            dma((2, 2, 6)), dma((2, 2, 6)), dma((NU,)), dma((NU,)), dma((4,)), dma((4,)),
            dma((ND,)), dma((ND,)), dma((NU,)), dma((NU,)),
        ],
        compiler_params=pltpu.CompilerParams(
            collective_id=0, has_side_effects=True, vmem_limit_bytes=62 * 1024 * 1024
        ),
    )(tok, dout, begins, cos, sin, gain, wqkv, wout)


def body(tokens, d_out, lengths, gain, w_qkv, w_out):
    u = lax.axis_index("ulysses")
    d = lax.axis_index("dp")
    begins, places = doc_positions(lengths[0], SEQ)
    cos_t, sin_t = rotary_tables_t(places)
    d_tokens, grad_qkv, grad_out, gain_sum = block_step(
        tokens[0], d_out[0], begins[None, :], cos_t, sin_t, gain[None, :], w_qkv, w_out
    )
    grad_gain = lax.dynamic_slice(gain_sum, (u, d * 16), (1, 16)).reshape(16)
    return d_tokens[None], grad_qkv, grad_out, grad_gain


def solution(mesh):
    in_specs = (
        P("dp", "ulysses", None),
        P("dp", "ulysses", None),
        P("dp", None),
        P("dp"),
        P("dp", None),
        P("dp", None),
    )
    out_specs = (
        P("dp", "ulysses", None),
        P(("ulysses", "dp"), None),
        P(("ulysses", "dp"), None),
        P(("ulysses", "dp")),
    )
    return jax.shard_map(body, mesh=mesh, in_specs=in_specs, out_specs=out_specs, check_vma=False)
```

```python
import math

import jax
import jax.numpy as jnp
from jax import lax
from jax.experimental import pallas as pl
from jax.experimental.pallas import tpu as pltpu
from jax.sharding import PartitionSpec as P

HEADS = 16
KV_HEADS = 4
HEAD_DIM = 64
D = 2048
SEQ = 2048
ROWS = 256
QW = 1024
KW = 256
NU = 8
ND = 16
EPS = 1e-05
ROPE_BASE = 500000.0
MESH = pl.DeviceIdType.MESH
F32 = jnp.float32
BF16 = jnp.bfloat16


def doc_positions(doc_lengths, length):
    order = jnp.arange(doc_lengths.shape[0])
    bounds = jnp.sum(jnp.where(order[None, :] < order[:, None], doc_lengths[None, :], 0), axis=1)
    places = jnp.arange(length, dtype=jnp.int32)
    begins = jnp.max(jnp.where(bounds[None, :] <= places[:, None], bounds[None, :], 0), axis=1)
    return begins, places - begins


def rotary_tables_t(places):
    inverse = ROPE_BASE ** (-jnp.arange(0, HEAD_DIM, 2).astype(F32) / HEAD_DIM)
    angles = inverse[:, None] * places.astype(F32)[None, :]
    return jnp.cos(angles), jnp.sin(angles)


def remote(src, dst, send_sem, recv_sem, u, d):
    return pltpu.make_async_remote_copy(
        src_ref=src, dst_ref=dst, send_sem=send_sem, recv_sem=recv_sem,
        device_id={"ulysses": u, "dp": d}, device_id_type=MESH,
    )


QB = 128
WIN = 512
FACTOR = 1.0 / math.sqrt(SEQ * ND)
HALF = 80
PART = 40


def rot_t(u, cos, sin):
    a, b = u[: HEAD_DIM // 2], u[HEAD_DIM // 2 :]
    return jnp.concatenate([a * cos - b * sin, b * cos + a * sin], axis=0)


def step_kernel(tok, dout, begins, cos, sin, gain_in, wqkv, wout,
                dtok_o, gqkv_o, gout_o, ggain_o,
                T, N, G, W, WO, GN, gain_rows, gain, WS, q_t, kv_t, kv, da_t, attn_t, dq_t, dq, dkv, acc,
                DP, RKV, OT, KVS, KVT, R, B1, B2, FIN, FKV, DN, gbuf, GR, gsum, GU,
                zs, zr, ps, pr, ws, wr, os_, or_, gns, gnr, wps, wpr, loc,
                ms, mr, qs, qr, ks, kr, rs, rr, fs, fr, vs, vr, gs, gr, us, ur):
    u = lax.axis_index("ulysses")
    d = lax.axis_index("dp")
    z, c = u // 2, u % 2
    x, y = d // 4, d % 4
    right = ((z + 1) % 4) * 2 + c
    left = ((z + 3) % 4) * 2 + c
    far = ((z + 2) % 4) * 2 + c
    mate = z * 2 + (1 - c)

    gain_rows[...] = jnp.broadcast_to(gain_in[...].astype(F32), (8, 128))
    barrier = pltpu.get_barrier_semaphore()

    @pl.loop(1, NU)
    def _(k):
        pl.semaphore_signal(barrier, inc=1, device_id={"ulysses": (u + k) % NU, "dp": d}, device_id_type=MESH)

    @pl.loop(1, ND)
    def _(k):
        pl.semaphore_signal(barrier, inc=1, device_id={"ulysses": u, "dp": (d + k) % ND}, device_id_type=MESH)

    pl.semaphore_wait(barrier, NU + ND - 2)

    H = ROWS // 2
    A, B = pl.ds(0, H), pl.ds(H, H)
    srcs, dsts = (tok, dout), (T, G)

    def own(a, slot, rows, to):
        return remote(srcs[a].at[rows], dsts[a].at[u, rows], zs.at[a, slot], zr.at[a, slot], to, d)

    def fwd(a, slot, frm, rows, to):
        return remote(dsts[a].at[frm, rows], dsts[a].at[frm, rows], zs.at[a, slot], zr.at[a, slot], to, d)

    def relay(a, slot, frm, rows):
        return remote(dsts[a].at[frm, rows], dsts[a].at[frm, rows], ps.at[a, slot], pr.at[a, slot], mate, d)

    def own_relay(a):
        return remote(srcs[a], dsts[a].at[u], ps.at[a, 6], pr.at[a, 6], mate, d)

    def start_own(a):
        own(a, 0, A, right).start()
        own(a, 3, B, left).start()
        own(a, 1, B, right).start()
        own(a, 2, A, left).start()
        own_relay(a).start()

    start_own(0)

    def along_x(h, st):
        return (h == 0) == (st == 0)

    def near(h, st, step):
        if along_x(h, st):
            return ((x + step) % 4) * 4 + y
        return x * 4 + (y + step) % 4

    def w_piece(h, st, step, part):
        rows = pl.ds(h * 32 + part * 16, 16)
        if along_x(h, st):
            j = (x + step) % 4
            return W.at[j, y, c, rows] if st == 0 else W.at[j, :, c, rows]
        j = (y + step) % 4
        return W.at[x, j, c, rows] if st == 0 else W.at[:, j, c, rows]

    W_ROUTE = ((0, 0, 1), (0, 1, 3), (0, 1, 1), (0, 0, 3), (3, 0, 1), (1, 1, 3))

    def w_copy(h, st, slot):
        step, part, to = W_ROUTE[slot]
        if st == 0 and step == 0:
            src = wqkv.at[pl.ds(c * 64 + h * 32 + part * 16, 16)]
        else:
            src = w_piece(h, st, step, part)
        return remote(src, w_piece(h, st, step, part), ws.at[h, st, slot], wr.at[h, st, slot], u, near(h, st, to))

    def w_start(h, st):
        for slot in range(4):
            w_copy(h, st, slot).start()

    def w_pass(h, st):
        for slot in range(2):
            w_copy(h, st, slot).wait_recv()
            w_copy(h, st, slot + 4).start()

    def w_end(h, st):
        for slot in range(2, 6):
            w_copy(h, st, slot).wait_recv()

    def o_copy(k):
        to = (d + k) % ND
        return remote(wout.at[:, pl.ds(pl.multiple_of(u * 128, 128), 128)], WO.at[d], os_.at[k], or_.at[k], u, to)

    def gain_copy(k):
        to = (d + k) % ND
        return remote(gain_rows, GN.at[d], gns.at[k], gnr.at[k], u, to)

    w_local = pltpu.make_async_copy(wqkv.at[pl.ds(c * 64, 64)], W.at[x, y, c], loc)
    w_local.start()
    w_start(0, 0)
    w_start(1, 0)

    @pl.loop(1, ND)
    def _(k):
        gain_copy(k).start()

    T[u] = tok[...]
    G[u] = dout[...]
    GN[d] = gain_rows[...]
    WO[d] = wout[:, pl.ds(pl.multiple_of(u * 128, 128), 128)]

    def arrivals(a):
        own(a, 0, A, right).wait_recv()
        fwd(a, 4, left, A, right).start()
        relay(a, 0, left, A).start()
        own(a, 3, B, left).wait_recv()
        fwd(a, 5, right, B, left).start()
        relay(a, 3, right, B).start()

    def late(a):
        own(a, 1, B, right).wait_recv()
        relay(a, 1, left, B).start()
        own(a, 2, A, left).wait_recv()
        relay(a, 2, right, A).start()

    def last(a):
        fwd(a, 4, far, A, right).wait_recv()
        relay(a, 4, far, A).start()
        fwd(a, 5, far, B, left).wait_recv()
        relay(a, 5, far, B).start()

    def norm(ch):
        @pl.loop(0, ROWS // 32)
        def _(r):
            rows = pl.ds(pl.multiple_of(r * 32, 32), 32)
            wide = T[ch, rows, :].astype(F32)
            inv = lax.rsqrt(jnp.mean(wide * wide, axis=1, keepdims=True) + EPS)
            N[ch, rows, :] = (wide * inv * gain[...]).astype(BF16)

    def chunk_cols(ch):
        return pl.ds(pl.multiple_of(ch * ROWS, ROWS), ROWS)

    def project(ch):
        cols = chunk_cols(ch)
        proj_t = jnp.dot(N[ch], WS[...], preferred_element_type=F32).T
        cos_, sin_ = cos[:, cols], sin[:, cols]
        q_t[0:64, cols] = rot_t(proj_t[0:64], cos_, sin_).astype(BF16)
        q_t[64:128, cols] = rot_t(proj_t[64:128], cos_, sin_).astype(BF16)
        both = jnp.concatenate([rot_t(proj_t[128:192], cos_, sin_), proj_t[192:256]], axis=0)
        kv_t[:, cols] = both.astype(BF16)
        kv[cols, :] = both.T.astype(BF16)

    def attend(*blocks):
        for i in blocks:
            da_t[:, pl.ds(pl.multiple_of(i * QB, QB), QB)] = jnp.dot(
                G[i // 2, pl.ds(pl.multiple_of((i % 2) * QB, QB), QB), :], WO[...].reshape(D, 128),
                preferred_element_type=F32,
            ).T.astype(BF16)
        for i in blocks:
            attend_block(i)

    def attend_block(i):
        start = pl.multiple_of(jnp.maximum(i - 3, 0) * QB, QB)
        here = pl.ds(pl.multiple_of(i * QB, QB), QB)
        keys = kv[pl.ds(start, WIN), :]
        keys_t = kv_t[:, pl.ds(start, WIN)]
        q = (q_t[:, here].astype(F32) * (HEAD_DIM ** -0.5)).astype(BF16)
        da = da_t[:, here]
        none = jnp.zeros((64, 2 * QB), BF16)
        q2 = jnp.concatenate([q[0:64], q[64:128]], axis=1)
        da2 = jnp.concatenate([da[0:64], da[64:128]], axis=1)
        mixed = jnp.concatenate(
            [jnp.concatenate([q2, none], axis=1), jnp.concatenate([none, da2], axis=1)], axis=0
        )
        st = jnp.dot(keys, mixed, preferred_element_type=F32)
        key_pos = start + lax.broadcasted_iota(jnp.int32, (WIN, QB), 0)
        query_pos = i * QB + lax.broadcasted_iota(jnp.int32, (WIN, QB), 1)
        allowed = (key_pos >= begins[:, here]) & (key_pos <= query_pos)
        s = jnp.concatenate(
            [jnp.where(allowed, st[:, 0:QB], -1e30), jnp.where(allowed, st[:, QB : 2 * QB], -1e30)], axis=1
        )
        w = jnp.exp(s - jnp.max(s, axis=0, keepdims=True))
        p = w * (1.0 / jnp.sum(w, axis=0, keepdims=True))
        pb = p.astype(BF16)
        o = jnp.dot(keys_t, pb, preferred_element_type=F32)[64:128]
        delta = jnp.sum(da2.astype(F32) * o, axis=0, keepdims=True)
        ds = (p * (st[:, 2 * QB :] - delta)).astype(BF16)
        g = jnp.dot(keys_t, ds, preferred_element_type=F32)[0:64] * (HEAD_DIM ** -0.5)
        attn_t[0:64, here] = o[:, 0:QB].astype(BF16)
        attn_t[64:128, here] = o[:, QB:].astype(BF16)
        cos_, sin_ = cos[:, here], -sin[:, here]
        turned = jnp.concatenate([rot_t(g[:, 0:QB], cos_, sin_), rot_t(g[:, QB:], cos_, sin_)], axis=0)
        dq_t[:, here] = turned.astype(BF16)
        dq[here, :] = turned.T.astype(BF16)
        acc[pl.ds(start, WIN), :] += lax.dot_general(
            jnp.concatenate([ds, pb], axis=1), mixed, (((1,), (1,)), ((), ())), preferred_element_type=F32
        )

    acc[...] = jnp.zeros_like(acc)

    w_pass(0, 0)
    w_pass(1, 0)
    w_local.wait()
    for h in range(2):
        w_end(h, 0)
        w_start(h, 1)

    @pl.loop(1, ND)
    def _(k):
        gain_copy(k).wait()
        o_copy(k).start()

    for i in range(ND):
        gain[:, i * 128 : (i + 1) * 128] = GN[i, 0:1, :]
    norm(u)
    arrivals(0)
    start_own(1)
    own_relay(0).wait_recv()
    norm(mate)
    w_pass(0, 1)
    w_pass(1, 1)
    w_end(0, 1)
    w_end(1, 1)
    w_mate = remote(W.at[:, :, c], W.at[:, :, c], wps, wpr, mate, d)
    w_mate.start()
    late(0)

    @pl.loop(0, 2)
    def _(n):
        norm(((z + 1 + 2 * n) % 4) * 2 + c)

    last(0)
    for slot, rows in ((0, A), (1, B), (2, A), (3, B)):
        relay(0, slot, left, rows).wait_recv()

    @pl.loop(0, 3)
    def _(n):
        norm(jnp.where(n == 2, far, ((z + 1 + 2 * n) % 4) * 2 + (1 - c)))

    w_mate.wait()
    WS[:, 0:128] = W[:, :, :, :, pl.ds(pl.multiple_of(u * 128, 128), 128)].reshape(D, 128)
    k_tile = W[:, :, :, :, pl.ds(pl.multiple_of(QW + (z // 2) * 128, 128), 128)].reshape(D, 128)
    v_tile = W[:, :, :, :, pl.ds(pl.multiple_of(QW + KW + (z // 2) * 128, 128), 128)].reshape(D, 128)

    @pl.when(z % 2 == 0)
    def _():
        WS[:, 128:256] = jnp.concatenate([k_tile[:, 0:64], v_tile[:, 0:64]], axis=1)

    @pl.when(z % 2 == 1)
    def _():
        WS[:, 128:256] = jnp.concatenate([k_tile[:, 64:], v_tile[:, 64:]], axis=1)

    relay(0, 4, far, A).wait_recv()
    relay(0, 5, far, B).wait_recv()
    norm(((z + 2) % 4) * 2 + (1 - c))

    @pl.loop(0, NU)
    def _(n):
        project(n)

    @pl.loop(1, ND)
    def _(k):
        o_copy(k).wait()

    arrivals(1)
    own_relay(1).wait_recv()

    @pl.loop(0, 2)
    def _(n):
        attend((z * 2 + n) * 2, (z * 2 + n) * 2 + 1)

    def attend_near(first):
        @pl.loop(0, 2)
        def _(n):
            base = ((z + 3 + 2 * n) % 4) * 4
            half = n if first else 1 - n
            attend(base + half, base + 2 + half)

    relay(1, 0, left, A).wait_recv()
    relay(1, 3, left, B).wait_recv()
    attend_near(True)
    late(1)
    relay(1, 1, left, B).wait_recv()
    relay(1, 2, left, A).wait_recv()
    attend_near(False)

    def dw(f, steps, add):
        cols = pl.ds(pl.multiple_of(f * 256, 256), 256)
        q = o = 0.0
        for step in steps:
            zz = (z + step) % 4
            toks = pl.ds(pl.multiple_of(zz * 512, 512), 512)
            q += jnp.dot(dq_t[:, toks], N[pl.ds(zz * 2, 2), :, cols].reshape(512, 256), preferred_element_type=F32)
            o += jnp.dot(attn_t[:, toks], G[pl.ds(zz * 2, 2), :, cols].reshape(512, 256), preferred_element_type=F32)
        rows = pl.ds(pl.multiple_of(f * 16, 16), 16)
        both = jnp.concatenate([q.T, o.T], axis=1).reshape(4, 4, 16, 256)
        R[:, :, rows, :] = R[:, :, rows, :] + both if add else both

    @pl.loop(0, NU)
    def _(f):
        dw(f, (0, 1, 3), False)

    last(1)

    @pl.loop(0, 2)
    def _(n):
        @pl.when(n == 1)
        def _():
            relay(1, 4, far, A).wait_recv()
            relay(1, 5, far, B).wait_recv()

        ch = ((z + 2) % 4) * 2 + (c + n) % 2
        attend(ch * 2, ch * 2 + 1)

    @pl.loop(0, NU)
    def _(b):
        cols = chunk_cols(b)
        t = acc[cols, :].T
        t = jnp.concatenate([rot_t(t[0:64], cos[:, cols], -sin[:, cols]), t[64:128]], axis=0)
        dkv[cols, :] = t.T.astype(BF16)

    def q_copy(k):
        to = (u + k) % NU
        rows = pl.ds(pl.multiple_of(to * ROWS, ROWS), ROWS)
        cols = pl.ds(pl.multiple_of(u * 128, 128), 128)
        return remote(dq.at[rows], DP.at[:, cols], qs.at[k], qr.at[k], to, d)

    def kv_copy(k):
        to = (u + k) % NU
        rows = pl.ds(pl.multiple_of(to * ROWS + c * 128, 128), 128)
        return remote(KVS.at[rows], RKV.at[z, pl.ds(pl.multiple_of(c * 128, 128), 128)], ks.at[k], kr.at[k], to, d)

    m_copy = remote(dkv, OT, ms, mr, mate, d)
    m_copy.start()

    @pl.loop(1, NU)
    def _(k):
        q_copy(k).start()

    DP[:, pl.ds(pl.multiple_of(u * 128, 128), 128)] = dq[pl.ds(pl.multiple_of(u * ROWS, ROWS), ROWS), :]

    def piece(h, st, step, part):
        rows = pl.ds(h * HALF, HALF) if st == 1 else pl.ds(h * HALF + part * PART, PART)
        if along_x(h, st):
            j = (x + step) % 4
            return R.at[j, :, rows, :] if st == 0 else R.at[j, y, rows, :]
        j = (y + step) % 4
        return R.at[:, j, rows, :] if st == 0 else R.at[x, j, rows, :]

    def buf(h, st, slot):
        return B1.at[h, slot] if st == 0 else B2.at[h, slot]

    ROUTE = ((2, 0, 1), (2, 1, 3), (1, 1, 1), (3, 0, 3), (1, 0, 1), (3, 1, 3))

    def rcp(h, st, slot):
        if st == 1:
            step = slot + 1
            return remote(piece(h, 1, step, 0), buf(h, 1, slot), rs.at[h, 1, slot], rr.at[h, 1, slot], u, near(h, 1, step))
        step, part, to = ROUTE[slot]
        return remote(piece(h, st, step, part), buf(h, st, slot), rs.at[h, st, slot], rr.at[h, st, slot],
                      u, near(h, st, to))

    def start(h, st):
        for slot in range(4 if st == 0 else 3):
            rcp(h, st, slot).start()

    def pass_on(h, st):
        for slot, step, part in ((0, 1, 0), (1, 3, 1)):
            rcp(h, st, slot).wait_recv()
            p = piece(h, st, step, part)
            p[...] = p[...] + buf(h, st, slot)[...]
            rcp(h, st, slot + 4).start()

    def gather_up(h, st):
        if st == 1:
            for slot in range(3):
                rcp(h, 1, slot).wait_recv()
            p = piece(h, 1, 0, 0)
            p[...] = p[...] + (buf(h, 1, 0)[...] + buf(h, 1, 1)[...] + buf(h, 1, 2)[...])
            return
        for part, one, two in ((0, 3, 4), (1, 2, 5)):
            rcp(h, st, one).wait_recv()
            rcp(h, st, two).wait_recv()
            p = piece(h, st, 0, part)
            p[...] = p[...] + (buf(h, st, one)[...] + buf(h, st, two)[...])

    @pl.loop(0, 5)
    def _(f):
        dw(f, (2,), True)

    start(0, 0)

    @pl.loop(5, NU)
    def _(f):
        dw(f, (2,), True)

    m_copy.wait()

    @pl.loop(0, NU)
    def _(b):
        rows = pl.ds(pl.multiple_of(b * ROWS, ROWS), ROWS)
        both = (dkv[rows, :].astype(F32) + OT[rows, :].astype(F32)).astype(BF16)
        KVS[rows, :] = both
        KVT[:, rows] = both.astype(F32).T.astype(BF16)

    @pl.loop(1, NU)
    def _(k):
        kv_copy(k).start()

    RKV[z, pl.ds(pl.multiple_of(c * 128, 128), 128), :] = KVS[
        pl.ds(pl.multiple_of(u * ROWS + c * 128, 128), 128), :
    ]

    for i in range(4):
        cols = pl.ds(pl.multiple_of((c * 4 + i) * 256, 256), 256)
        kvp = jnp.dot(KVT[...], N[:, :, cols].reshape(SEQ, 256), preferred_element_type=F32)
        R[:, :, 128 + (i // 2) * 16 : 144 + (i // 2) * 16, (i % 2) * 128 : (i % 2) * 128 + 128] = (
            kvp.T.reshape(4, 4, 16, 128)
        )

    start(1, 0)
    pass_on(0, 0)
    pass_on(1, 0)

    @pl.loop(1, NU)
    def _(k):
        q_copy(k).wait()
        kv_copy(k).wait()

    for i in range(2):
        a, b = RKV[2 * i], RKV[2 * i + 1]
        DP[:, QW + i * 128 : QW + (i + 1) * 128] = jnp.concatenate([a[:, 0:64], b[:, 0:64]], axis=1)
        DP[:, QW + KW + i * 128 : QW + KW + (i + 1) * 128] = jnp.concatenate([a[:, 64:], b[:, 64:]], axis=1)

    wide = tok[...].astype(F32)
    inv = lax.rsqrt(jnp.mean(wide * wide, axis=1, keepdims=True) + EPS)

    def back(f, along):
        cols = pl.ds(pl.multiple_of(f * 256, 256), 256)
        dn = lax.dot_general(DP[...], W[f // 2, pl.ds((f % 2) * 2, 2)].reshape(256, QW + 2 * KW), (((1,), (1,)), ((), ())), preferred_element_type=F32)
        unit = tok[:, cols].astype(F32) * inv
        gbuf[pl.ds(f, 1), :] = jnp.sum(dn * unit, axis=0, keepdims=True)
        scaled = dn * gain[:, cols]
        DN[f] = scaled
        return along + jnp.sum(scaled * unit, axis=1, keepdims=True)

    along = lax.fori_loop(0, NU, back, jnp.zeros((ROWS, 1), F32))
    mean = along * (1.0 / D)

    def g_copy(k):
        return remote(gbuf, GR.at[d], gs.at[k], gr.at[k], u, (d + k) % ND)

    @pl.loop(1, ND)
    def _(k):
        g_copy(k).start()

    GR[d] = gbuf[...]

    gather_up(0, 0)
    start(0, 1)
    gather_up(1, 0)
    start(1, 1)

    @pl.loop(0, NU)
    def _(f):
        cols = pl.ds(pl.multiple_of(f * 256, 256), 256)
        unit = tok[:, cols].astype(F32) * inv
        d_rows = inv * (DN[f] - unit * mean)
        dtok_o[:, cols] = (dout[:, cols].astype(F32) + d_rows).astype(BF16)


    @pl.loop(1, ND)
    def _(k):
        g_copy(k).wait()

    gsum[...] = jnp.sum(GR[...], axis=0)

    def gu_copy(k):
        return remote(gsum, GU.at[u], us.at[k], ur.at[k], (u + k) % NU, d)

    @pl.loop(1, NU)
    def _(k):
        gu_copy(k).start()

    GU[u] = gsum[...]
    gather_up(0, 1)
    gather_up(1, 1)

    def f_copy(k):
        to = (u + k) % NU
        return remote(R.at[x, y, pl.ds(pl.multiple_of(to * 16, 16), 16)], FIN.at[u], fs.at[k], fr.at[k], to, d)

    @pl.loop(1, NU)
    def _(k):
        f_copy(k).start()

    def v_block(i):
        return R.at[x, y, pl.ds(128 + (i // 2) * 16, 16), pl.ds((i % 2) * 128, 128)]

    def v_copy(i):
        return remote(v_block(i), FKV.at[z], vs.at[i], vr.at[z], c * 4 + i, d)

    def v_arrival(zs):
        return remote(v_block(0), FKV.at[zs], vs.at[0], vr.at[zs], u, d)

    for i in range(4):
        @pl.when(c * 4 + i != u)
        def _():
            v_copy(i).start()

        @pl.when(c * 4 + i == u)
        def _():
            FKV[z] = v_block(i)[...]

    FIN[u] = R[x, y, pl.ds(pl.multiple_of(u * 16, 16), 16), :]

    @pl.loop(1, NU)
    def _(k):
        gu_copy(k).wait()

    ggain_o[...] = jnp.sum(GU[...], axis=0) * FACTOR

    @pl.loop(1, NU)
    def _(k):
        f_copy(k).wait()

    for i in range(4):
        @pl.when(i * 2 + u // 4 != u)
        def _():
            v_arrival(i).wait_recv()

        @pl.when(c * 4 + i != u)
        def _():
            v_copy(i).wait_send()

    for i in range(NU):
        gqkv_o[:, i * 128 : (i + 1) * 128] = FIN[i, :, 0:128] * FACTOR
        gout_o[:, i * 128 : (i + 1) * 128] = FIN[i, :, 128:256] * FACTOR
    for i in range(2):
        a, b = FKV[2 * i] * FACTOR, FKV[2 * i + 1] * FACTOR
        gqkv_o[:, QW + i * 128 : QW + (i + 1) * 128] = jnp.concatenate([a[:, 0:64], b[:, 0:64]], axis=1)
        gqkv_o[:, QW + KW + i * 128 : QW + KW + (i + 1) * 128] = jnp.concatenate([a[:, 64:], b[:, 64:]], axis=1)

    for h in range(2):
        for st in range(2):
            for slot in range(6 if st == 0 else 3):
                rcp(h, st, slot).wait_send()


    for h in range(2):
        for st in range(2):
            for slot in range(6):
                w_copy(h, st, slot).wait_send()
    for a in range(2):
        own(a, 0, A, right).wait_send()
        own(a, 1, B, right).wait_send()
        own(a, 2, A, left).wait_send()
        own(a, 3, B, left).wait_send()
        fwd(a, 4, left, A, right).wait_send()
        fwd(a, 5, right, B, left).wait_send()
        own_relay(a).wait_send()
        relay(a, 0, left, A).wait_send()
        relay(a, 1, left, B).wait_send()
        relay(a, 2, right, A).wait_send()
        relay(a, 3, right, B).wait_send()
        relay(a, 4, far, A).wait_send()
        relay(a, 5, far, B).wait_send()


def block_step(tok, dout, begins, cos, sin, gain, wqkv, wout):
    dma = pltpu.SemaphoreType.DMA
    vmem = pl.BlockSpec(memory_space=pltpu.VMEM)
    V = pltpu.VMEM
    return pl.pallas_call(
        step_kernel,
        name="block_step",
        out_shape=(
            jax.ShapeDtypeStruct((ROWS, D), BF16),
            jax.ShapeDtypeStruct((16, QW + 2 * KW), F32),
            jax.ShapeDtypeStruct((16, QW), F32),
            jax.ShapeDtypeStruct((NU, 256), F32),
        ),
        in_specs=[vmem] * 8,
        out_specs=(vmem,) * 4,
        scratch_shapes=[
            V((NU, ROWS, D), BF16), V((NU, ROWS, D), BF16), V((NU, ROWS, D), BF16),
            V((4, 4, 2, 64, QW + 2 * KW), BF16), V((ND, 128, 128), BF16), V((ND, 8, 128), F32),
            V((8, 128), F32), V((1, D), F32), V((D, 256), BF16),
            V((128, SEQ), BF16), V((128, SEQ), BF16), V((SEQ, 128), BF16), V((128, SEQ), BF16),
            V((128, SEQ), BF16), V((128, SEQ), BF16), V((SEQ, 128), BF16), V((SEQ, 128), BF16),
            V((SEQ, 128), F32),
            V((ROWS, QW + 2 * KW), BF16), V((4, ROWS, 128), BF16),
            V((SEQ, 128), BF16), V((SEQ, 128), BF16), V((128, SEQ), BF16),
            V((4, 4, 2 * HALF, 256), F32), V((2, 6, 4, PART, 256), F32), V((2, 3, HALF, 256), F32),
            V((NU, 16, 256), F32), V((4, 16, 128), F32), V((NU, ROWS, 256), F32),
            V((NU, 256), F32), V((ND, NU, 256), F32), V((NU, 256), F32), V((NU, NU, 256), F32),
            dma((2, 6)), dma((2, 6)), dma((2, 7)), dma((2, 7)), dma((2, 2, 6)), dma((2, 2, 6)),
            dma((ND,)), dma((ND,)), dma((ND,)), dma((ND,)), dma, dma, dma,
            dma, dma, dma((NU,)), dma((NU,)), dma((NU,)), dma((NU,)),
            dma((2, 2, 6)), dma((2, 2, 6)), dma((NU,)), dma((NU,)), dma((4,)), dma((4,)),
            dma((ND,)), dma((ND,)), dma((NU,)), dma((NU,)),
        ],
        compiler_params=pltpu.CompilerParams(
            collective_id=0, has_side_effects=True, vmem_limit_bytes=62 * 1024 * 1024
        ),
    )(tok, dout, begins, cos, sin, gain, wqkv, wout)


def body(tokens, d_out, lengths, gain, w_qkv, w_out):
    u = lax.axis_index("ulysses")
    d = lax.axis_index("dp")
    begins, places = doc_positions(lengths[0], SEQ)
    cos_t, sin_t = rotary_tables_t(places)
    d_tokens, grad_qkv, grad_out, gain_sum = block_step(
        tokens[0], d_out[0], begins[None, :], cos_t, sin_t, gain[None, :], w_qkv, w_out
    )
    grad_gain = lax.dynamic_slice(gain_sum, (u, d * 16), (1, 16)).reshape(16)
    return d_tokens[None], grad_qkv, grad_out, grad_gain


def solution(mesh):
    in_specs = (
        P("dp", "ulysses", None),
        P("dp", "ulysses", None),
        P("dp", None),
        P("dp"),
        P("dp", None),
        P("dp", None),
    )
    out_specs = (
        P("dp", "ulysses", None),
        P(("ulysses", "dp"), None),
        P(("ulysses", "dp"), None),
        P(("ulysses", "dp")),
    )
    return jax.shard_map(body, mesh=mesh, in_specs=in_specs, out_specs=out_specs, check_vma=False)
```
